256 devices in a mesh: neuron: 64 (over z, x_hi, y), tm: 4 (over x_lo, core).
Axes of the slice: x: 4 (x_hi: 2, x_lo: 2; x = x_hi * 2 + x_lo), y: 4, z: 8, core: 2. Of those that a mesh axis runs over, the one named last changes fastest.
Arguments:
- data: bfloat16 [8192, 8192], P('neuron', 'tm'), may hold values from 0 to 2
- behaviour: bfloat16 [512, 8192], P('neuron', 'tm'), may hold values from 0 to 2
- motifs: bfloat16 [32, 8192, 128], P('tm', 'neuron'), may hold values from 0 to 2
- behav_motifs: bfloat16 [32, 512, 128], P('tm', 'neuron'), may hold values from 0 to 2
- activations: bfloat16 [128, 8192], P(None, 'tm'), may hold values from 0 to 2
Outputs:
- new_motifs: bfloat16 [32, 8192, 128], P('tm', 'neuron')
- new_behav_motifs: bfloat16 [32, 512, 128], P('tm', 'neuron')
- new_activations: bfloat16 [128, 8192], P(None, 'tm')
The draws below stay inside these ranges and needn't reach their ends.
All inputs are finite; a program needn't handle non-finite values.
Results may differ from the reference program's by a relative error of at most 0.0034.
Values may be sent and summed in bfloat16 or wider, within the bound.
No kernel may reach another device: no remote copies, remote signals or barrier semaphores. Data moves between devices by JAX's collectives and lax.ppermute only.
A program may use at most 64 MiB of HBM per device.

```python
import math
import jax
import jax.numpy as jnp
from jax import lax

K = 128
L = 32
F = 512
NN = 8192
NT = 8192


def levels(own_key, extent, pieces, least, largest):
    gain, own = 1.0, jax.random.fold_in(own_key, 6)
    for axis_at, blocks in pieces:
        heights = jnp.exp(jax.random.uniform(jax.random.fold_in(own, axis_at), (blocks,), jnp.float32, least / len(pieces), largest / len(pieces)))
        gain = gain * jnp.repeat(heights, extent[axis_at] // blocks).reshape([-1 if axis == axis_at else 1 for axis in range(len(extent))])
    return gain


def setup_inputs(seed: int = 0) -> dict:
    keys = jax.random.split(jax.random.key(seed), 6)
    return {
        "data": jnp.clip(2.0 * jax.random.uniform(keys[0], (NN, NT), jnp.float32) ** levels(keys[0], (NN, NT), ((0, 64), (1, 4)), -0.2, 0.2), 0.0, 2.0).astype(jnp.bfloat16),
        "behaviour": jnp.clip(2.0 * jax.random.uniform(keys[1], (F, NT), jnp.float32) ** levels(keys[1], (F, NT), ((0, 64), (1, 4)), -0.2, 0.2), 0.0, 2.0).astype(jnp.bfloat16),
        "motifs": jnp.clip(2.0 * jax.random.uniform(keys[2], (L, NN, K), jnp.float32) ** levels(keys[2], (L, NN, K), ((0, 4), (1, 64)), -0.2, 0.2), 0.0, 2.0).astype(jnp.bfloat16),
        "behav_motifs": jnp.clip(2.0 * jax.random.uniform(keys[3], (L, F, K), jnp.float32) ** levels(keys[3], (L, F, K), ((0, 4), (1, 64)), -0.2, 0.2), 0.0, 2.0).astype(jnp.bfloat16),
        "activations": jnp.clip(2.0 * jax.random.uniform(keys[4], (K, NT), jnp.float32) ** levels(keys[4], (K, NT), ((1, 4),), -0.2, 0.2), 0.0, 2.0).astype(jnp.bfloat16),
    }


def reference(data, behaviour, motifs, behav_motifs, activations):
    scale = 1.0 / (L * K)
    rate_motif = 0.5 * L * K / math.sqrt(NT)
    rate_active = 0.5 * L * K / math.sqrt(L * (NN + 4 * F))
    rim = L - 1
    extended = jnp.concatenate([jnp.zeros((K, rim), activations.dtype), activations], axis=1)
    lag_list = jnp.arange(L, dtype=jnp.int32)

    def window(lag):
        return lax.dynamic_slice_in_dim(extended, rim - lag, NT, 1)

    def forward(acc, lag):
        win = window(lag)
        neuron_rows = lax.dynamic_index_in_dim(motifs, lag, 0, keepdims=False)
        feature_rows = lax.dynamic_index_in_dim(behav_motifs, lag, 0, keepdims=False)
        return ((acc[0] + jnp.dot(neuron_rows, win, preferred_element_type=jnp.float32), acc[1] + jnp.dot(feature_rows, win, preferred_element_type=jnp.float32)), None)
    start_pair = (jnp.zeros((NN, NT), jnp.float32), jnp.zeros((F, NT), jnp.float32))
    (recon_x, recon_b), _ = lax.scan(forward, start_pair, lag_list)
    resid_x = (data.astype(jnp.float32) - scale * recon_x).astype(jnp.bfloat16)
    resid_b = (2.0 * (behaviour.astype(jnp.float32) - scale * recon_b)).astype(jnp.bfloat16)

    def motif_grad(lag):
        win = window(lag)
        neuron_part = lax.dot_general(resid_x, win, (((1,), (1,)), ((), ())), preferred_element_type=jnp.float32)
        feature_part = lax.dot_general(resid_b, win, (((1,), (1,)), ((), ())), preferred_element_type=jnp.float32)
        return (-scale * neuron_part, -scale * feature_part)
    grad_w, grad_v = lax.map(motif_grad, lag_list)

    def backward(acc, lag):
        neuron_rows = lax.dynamic_index_in_dim(motifs, lag, 0, keepdims=False)
        feature_rows = lax.dynamic_index_in_dim(behav_motifs, lag, 0, keepdims=False)
        back = lax.dot_general(neuron_rows, resid_x, (((0,), (0,)), ((), ())), preferred_element_type=jnp.float32)
        back = back + lax.dot_general(feature_rows, resid_b, (((0,), (0,)), ((), ())), preferred_element_type=jnp.float32)
        place = rim - lag
        current = lax.dynamic_slice_in_dim(acc, place, NT, 1)
        return (lax.dynamic_update_slice_in_dim(acc, current + back, place, 1), None)
    extended_back, _ = lax.scan(backward, jnp.zeros((K, rim + NT), jnp.float32), lag_list)
    grad_h = -scale * extended_back[:, rim:]
    new_motifs = jnp.maximum(motifs.astype(jnp.float32) - rate_motif * grad_w, 0.0).astype(jnp.bfloat16)
    new_behav = jnp.maximum(behav_motifs.astype(jnp.float32) - rate_motif * grad_v, 0.0).astype(jnp.bfloat16)
    new_active = jnp.maximum(activations.astype(jnp.float32) - rate_active * grad_h, 0.0).astype(jnp.bfloat16)
    return (new_motifs, new_behav, new_active)
```

```python
import functools
import math

import jax
import jax.numpy as jnp
from jax import lax
from jax.experimental import pallas as pl
from jax.experimental.pallas import tpu as pltpu
from jax.sharding import PartitionSpec as P


behaviour_weight = 2.0
lane = 128
group = 4
deep, wide = 16, 4
patch = 32
f32 = jnp.float32
bf16 = jnp.bfloat16
VMEM = pl.BlockSpec(memory_space=pltpu.VMEM)


def along(shard, by):
    pairs = [(i, i + by) for i in range(4) if 0 <= i + by < 4]
    return lax.ppermute(shard, "tm", pairs)


def crossed(shard, mask):
    return lax.ppermute(shard, "tm", [(i, i ^ mask) for i in range(4)])


def around(shard, by):
    pairs = [(i * wide + y, i * wide + (y + by) % wide) for i in range(deep) for y in range(wide)]
    return lax.ppermute(shard, "neuron", pairs)


def exchanged(blocks):
    groups = [[i * wide + y for i in range(deep)] for y in range(wide)]
    return lax.all_to_all(blocks, "neuron", 0, 0, axis_index_groups=groups, tiled=True)


def place():
    me = lax.axis_index("neuron")
    return me // wide, me % wide


def moved(x, by):
    by = by % x.shape[1]
    return x if by == 0 else pltpu.roll(x, x.shape[1] - by, 1)


def tiles(width, step):
    at = 0
    while at < width:
        size = min(step, width - at)
        yield at, size
        at += size


def shift_activations(earlier_ref, active_ref, later_ref, stack_ref, ext_ref):
    motifs, frames = active_ref.shape
    width = stack_ref.shape[1]
    steps = stack_ref.shape[0] // motifs
    rows = 16
    ext_ref[:, :lane] = earlier_ref[...]
    ext_ref[:, lane : lane + frames] = active_ref[...]
    ext_ref[:, lane + frames :] = later_ref[...]

    def chunk(i, carry):
        at = pl.multiple_of(i * rows, rows)
        block = ext_ref[pl.ds(at, rows), :]
        for a in range(steps):
            by = lane - (group - 1) - group * a
            stack_ref[pl.ds(pl.multiple_of(a * motifs + at, rows), rows), :] = moved(block, by)[:, :width]
        return carry

    lax.fori_loop(0, motifs // rows, chunk, 0)


def forward_backward(scale, frames, *refs):
    stack_ref, data_ref, data_halo_ref, behav_ref, behav_halo_ref = refs[:5]
    w_parts, v_parts = refs[5:9], refs[9:13]
    grad_refs, resid_ref = refs[13:17], refs[17]
    w_ref, v_ref, out_ref, back_ref, few_ref, sum_ref = refs[18:]
    lags, neurons, motifs = w_ref.shape
    features = v_ref.shape[1]
    steps = lags // group
    width = frames + lane
    mine = lax.axis_index("tm")
    _, y = place()
    part = lags // 4
    for p in range(4):
        from_device = mine ^ p
        w_ref[pl.ds(from_device * part, part)] = w_parts[p][...]
        v_ref[pl.ds(from_device * part, part)] = v_parts[p][...]

    rows_w = [jnp.concatenate([w_ref[group * a + b] for a in range(steps)], axis=1) for b in range(group)]
    rows_v = jnp.concatenate(
        [v_ref[group * a : group * (a + 1)].reshape(group * features, motifs) for a in range(steps)], axis=1
    )
    left = jnp.concatenate(rows_w + [rows_v], axis=0)
    for at, size in tiles(width, 256):
        out_ref[:, at : at + size] = jnp.dot(left, stack_ref[:, at : at + size], preferred_element_type=f32)

    valid = mine < 3
    rows = 8

    def residual(i, carry):
        at = pl.multiple_of(i * rows, rows)
        total = None
        for b in range(group):
            term = moved(out_ref[pl.ds(pl.multiple_of(b * neurons + at, rows), rows), :], group - 1 - b)
            total = term if total is None else total + term
        own = data_ref[pl.ds(at, rows), :].astype(f32) - scale * total[:, :frames]
        halo = data_halo_ref[pl.ds(at, rows), :].astype(f32) - scale * total[:, frames:]
        halo = jnp.where(valid, halo, 0.0)
        resid_ref[pl.ds(at, rows), :] = jnp.concatenate([own, halo], axis=1).astype(bf16)
        return carry

    lax.fori_loop(0, neurons // rows, residual, 0)
    total = None
    for b in range(group):
        first = group * neurons + b * features
        term = moved(out_ref[first : first + features, :], group - 1 - b)
        total = term if total is None else total + term
    own = behaviour_weight * (behav_ref[...].astype(f32) - scale * total[:, :frames])
    halo = behaviour_weight * (behav_halo_ref[...].astype(f32) - scale * total[:, frames:])
    halo = jnp.where(valid, halo, 0.0)
    resid_few = jnp.concatenate([own, halo], axis=1).astype(bf16)
    resid_ref[neurons:, :] = resid_few

    rows = 16

    def chunk(i, carry):
        at = pl.multiple_of(i * rows, rows)
        block = resid_ref[pl.ds(at, rows), :]
        for a in range(steps):
            back_ref[pl.ds(pl.multiple_of(a * neurons + at, rows), rows), :] = moved(block, group * a)
        return carry

    lax.fori_loop(0, neurons // rows, chunk, 0)
    few = resid_few.astype(f32)
    for l in range(0, lags, 2):
        pair = jnp.concatenate([moved(few, l)[:, :frames], moved(few, l + 1)[:, :frames]], axis=0)
        few_ref[l * features : (l + 2) * features, :] = pair.astype(bf16)

    left = jnp.concatenate(
        [jnp.concatenate([w_ref[group * a + b].T for a in range(steps)], axis=1) for b in range(group)], axis=0
    )
    for at, size in tiles(width, 256):
        out_ref[: group * motifs, at : at + size] = jnp.dot(
            left, back_ref[:, at : at + size], preferred_element_type=f32
        )
    left = v_ref[...].reshape(lags * features, motifs).T
    for at, size in tiles(frames, 256):
        total = jnp.dot(left, few_ref[:, at : at + size], preferred_element_type=f32)
        for b in range(group):
            reach = out_ref[b * motifs : (b + 1) * motifs, at : at + size + lane]
            total = total + moved(reach, b)[:, :size]
        for i in range(motifs // patch):
            for j in range(size // lane):
                sum_ref[i * (frames // lane) + at // lane + j] = total[
                    patch * i : patch * (i + 1), lane * j : lane * (j + 1)
                ]
    for r in range(wide):
        peer = (y + r) % wide
        grad_refs[r][...] = sum_ref[pl.ds(peer * deep, deep)].astype(grad_refs[r].dtype)


def motif_gradients(frames, motifs, stack_ref, resid_ref, keep_ref, relay_ref, send_ref, left_ref):
    features = keep_ref.shape[1] - 128
    neurons = resid_ref.shape[0] - features
    steps = stack_ref.shape[0] // motifs
    width = frames + lane
    rows = 16
    mask = lax.broadcasted_iota(jnp.int32, (rows, width), 1) < frames

    def chunk(i, carry):
        at = pl.multiple_of(i * rows, rows)
        block = jnp.where(mask, resid_ref[pl.ds(at, rows), :].astype(f32), 0.0)
        for b in range(group):
            shifted = moved(block, b - (group - 1)).astype(bf16)
            left_ref[pl.ds(pl.multiple_of(b * neurons + at, rows), rows), :] = shifted
        return carry

    lax.fori_loop(0, neurons // rows, chunk, 0)
    block = jnp.where(mask[:features], resid_ref[neurons:, :].astype(f32), 0.0)
    left_ref[group * neurons :, :] = jnp.concatenate(
        [moved(block, b - (group - 1)) for b in range(group)], axis=0
    ).astype(bf16)
    mine = lax.axis_index("tm")
    span = steps * motifs // 4
    for p in (3, 1, 2, 0):
        first = pl.multiple_of((mine ^ p) * span, span)
        result = lax.dot_general(
            left_ref[...], stack_ref[pl.ds(first, span), :], (((1,), (1,)), ((), ())), preferred_element_type=f32
        )
        for a in range(span // motifs):
            for b in range(group):
                target = (keep_ref, send_ref.at[0], relay_ref, send_ref.at[1])[p]
                l = group * a + b
                cols = slice(a * motifs, (a + 1) * motifs)
                few = group * neurons + b * features
                target[l, :neurons, :] = result[b * neurons : (b + 1) * neurons, cols].astype(target.dtype)
                target[l, neurons:, :] = result[few : few + features, cols].astype(target.dtype)


def sum_around(*refs):
    parts, out_ref = refs[:wide], refs[wide]
    total = parts[0][...]
    for part in parts[1:]:
        total = total + part[...].astype(f32)
    out_ref[...] = total.astype(out_ref.dtype)


def update(factor, active_ref, parts_ref, out_ref):
    i, y = place()
    own = active_ref[pl.ds(pl.multiple_of(y * patch, patch), patch), pl.ds(pl.multiple_of(i * lane, lane), lane)]
    total = jnp.sum(parts_ref[...].astype(f32), axis=0)
    block = jnp.maximum(own.astype(f32) + factor * total, 0.0).astype(bf16)
    for j in range(deep):
        out_ref[j] = block


def join_columns(parts_ref, out_ref):
    for j in range(deep):
        out_ref[:, lane * j : lane * (j + 1)] = parts_ref[j]


def join_rows(*refs):
    parts, out_ref = refs[:wide], refs[wide]
    _, y = place()
    for r in range(wide):
        row = pl.multiple_of((y + wide - r) % wide * patch, patch)
        out_ref[pl.ds(row, patch), :] = parts[r][...]


def call(body, out_shape, scratch, args, flops=0, moves=1 << 20, vmem=8):
    return pl.pallas_call(
        body,
        out_shape=out_shape,
        in_specs=[VMEM] * len(args),
        out_specs=jax.tree.map(lambda _: VMEM, out_shape),
        scratch_shapes=scratch,
        compiler_params=pltpu.CompilerParams(vmem_limit_bytes=vmem << 20),
        cost_estimate=pl.CostEstimate(flops=flops, bytes_accessed=moves, transcendentals=0),
    )(*args)


def local(data, behaviour, motifs, behav_motifs, activations):
    lags_here, neurons, width = motifs.shape
    features = behaviour.shape[0]
    frames = activations.shape[1]
    lags = lags_here * lax.axis_size("tm")
    all_frames = frames * lax.axis_size("tm")
    all_neurons = neurons * lax.axis_size("neuron")
    all_features = features * lax.axis_size("neuron")
    scale = 1.0 / (lags * width)
    rate_motif = 0.5 * lags * width / math.sqrt(all_frames)
    rate_active = 0.5 * lags * width / math.sqrt(lags * (all_neurons + 4 * all_features))
    shape = jax.ShapeDtypeStruct
    steps = lags // group

    w2, v2 = crossed(motifs, 2), crossed(behav_motifs, 2)
    w1, v1 = crossed(motifs, 1), crossed(behav_motifs, 1)
    earlier = along(activations[:, frames - lane :], 1)
    heads = along(
        jnp.concatenate([data[:, :lane], activations[:, :lane], behaviour[:, :lane]], axis=0), -1
    )
    w3, v3 = crossed(w2, 1), crossed(v2, 1)
    stack = call(
        shift_activations,
        shape((steps * width, frames + lane), bf16),
        [pltpu.VMEM((width, frames + 2 * lane), bf16)],
        [earlier, activations, heads[neurons : neurons + width]],
        moves=16 << 20,
        vmem=8,
    )

    grads_and_more = call(
        functools.partial(forward_backward, scale, frames),
        [shape((deep, patch, lane), f32 if r == 0 else bf16) for r in range(wide)]
        + [shape((neurons + features, frames + lane), bf16)],
        [
            pltpu.VMEM((lags, neurons, width), bf16),
            pltpu.VMEM((lags, features, width), bf16),
            pltpu.VMEM((group * (neurons + features), frames + lane), f32),
            pltpu.VMEM((steps * neurons, frames + lane), bf16),
            pltpu.VMEM((lags * features, frames), bf16),
            pltpu.VMEM((deep * wide, patch, lane), f32),
        ],
        [stack, data, heads[:neurons], behaviour, heads[neurons + width :], motifs, w1, w2, w3, behav_motifs, v1, v2, v3],
        flops=4 * lags * (neurons + features) * width * frames,
        moves=4 << 20,
        vmem=30,
    )
    grads, resid = grads_and_more[:wide], grads_and_more[wide]
    around_parts = [grads[0]]
    for r in range(1, wide):
        around_parts.append(around(grads[r], r))

    per_lag = (lags_here, neurons + features, width)
    keep, relay, send = call(
        functools.partial(motif_gradients, frames, width),
        [shape(per_lag, f32), shape(per_lag, f32), shape((2,) + per_lag, f32)],
        [pltpu.VMEM((group * (neurons + features), frames + lane), bf16)],
        [stack, resid],
        flops=2 * lags * (neurons + features) * width * frames,
        moves=4 << 20,
        vmem=20,
    )
    got = crossed(send, 1)

    sums = call(sum_around, shape((deep, patch, lane), bf16), [], around_parts)
    relayed = crossed(relay + got[1], 2)
    blocks = call(
        functools.partial(update, rate_active * scale),
        shape((deep, patch, lane), bf16),
        [],
        [activations, exchanged(sums)],
    )
    strip = call(join_columns, shape((patch, frames), bf16), [], [exchanged(blocks)])
    new_active = call(
        join_rows,
        shape((width, frames), bf16),
        [],
        [strip] + [around(strip, r) for r in range(1, wide)],
    )

    total = keep + got[0] + relayed
    step = rate_motif * scale
    new_motifs = jnp.maximum(motifs.astype(f32) + step * total[:, :neurons], 0.0).astype(bf16)
    new_behav = jnp.maximum(behav_motifs.astype(f32) + step * total[:, neurons:], 0.0).astype(bf16)
    return (new_motifs, new_behav, new_active)


def solution(mesh):
    placed = (
        P("neuron", "tm"),
        P("neuron", "tm"),
        P("tm", "neuron", None),
        P("tm", "neuron", None),
        P(None, "tm"),
    )
    return jax.shard_map(
        local,
        mesh=mesh,
        in_specs=placed,
        out_specs=(P("tm", "neuron", None), P("tm", "neuron", None), P(None, "tm")),
        check_vma=False,
    )
```

```python
import functools
import math

import jax
import jax.numpy as jnp
from jax import lax
from jax.experimental import pallas as pl
from jax.experimental.pallas import tpu as pltpu
from jax.sharding import PartitionSpec as P


behaviour_weight = 2.0
lane = 128
group = 4
deep, wide = 16, 4
patch = 32
f32 = jnp.float32
bf16 = jnp.bfloat16
VMEM = pl.BlockSpec(memory_space=pltpu.VMEM)
HBM = pl.BlockSpec(memory_space=pltpu.HBM)


def crossed(shard, mask):
    return lax.ppermute(shard, "tm", [(i, i ^ mask) for i in range(4)])


def around(shard, by):
    pairs = [(i * wide + y, i * wide + (y + by) % wide) for i in range(deep) for y in range(wide)]
    return lax.ppermute(shard, "neuron", pairs)


def exchanged(blocks):
    groups = [[i * wide + y for i in range(deep)] for y in range(wide)]
    return lax.all_to_all(blocks, "neuron", 0, 0, axis_index_groups=groups, tiled=True)


def place():
    me = lax.axis_index("neuron")
    return me // wide, me % wide


def moved(x, by):
    by = by % x.shape[1]
    return x if by == 0 else pltpu.roll(x, x.shape[1] - by, 1)


def tiles(width, step):
    at = 0
    while at < width:
        size = min(step, width - at)
        yield at, size
        at += size


edge = 32
first_a, last_a, first_d, first_b = 64, 96, 128, 160
pack_rows = 168


def fetched(pairs, sems):
    copies = [pltpu.make_async_copy(source, target, sems.at[i]) for i, (source, target) in enumerate(pairs)]
    for copy in copies:
        copy.start()
    for copy in copies:
        copy.wait()


def pack(v_hbm, active_hbm, data_hbm, behav_hbm, out_ref, v_ref, head_ref, tail_ref, data_ref, behav_ref, sems):
    frames = active_hbm.shape[1]
    fetched(
        [
            (v_hbm, v_ref),
            (active_hbm.at[:, :lane], head_ref),
            (active_hbm.at[:, frames - lane :], tail_ref),
            (data_hbm.at[:, :lane], data_ref),
            (behav_hbm.at[:, :lane], behav_ref),
        ],
        sems,
    )
    out_ref[:first_a] = v_ref[...].reshape(first_a, lane)
    out_ref[first_a:last_a] = head_ref[...].T[:edge]
    out_ref[last_a:first_d] = tail_ref[...].T[lane - edge :]
    out_ref[first_d:first_b] = data_ref[...].T[:edge]
    out_ref[first_b:] = behav_ref[...]


def nearest(odd, near_ref, far_ref, rows):
    mine = lax.axis_index("tm")
    return jnp.where(mine % 2 == odd, near_ref[rows, :], far_ref[rows, :])


def shift_activations(near_ref, far_ref, active_hbm, stack_ref, ext_ref, sems):
    motifs, frames = active_hbm.shape
    width = stack_ref.shape[1]
    steps = stack_ref.shape[0] // motifs
    rows = 16

    def fetch(i):
        part = pl.ds(pl.multiple_of(i * rows, rows), rows)
        return pltpu.make_async_copy(active_hbm.at[part], ext_ref.at[part, lane : lane + frames], sems.at[i])

    for i in range(motifs // rows):
        fetch(i).start()
    blank = jnp.zeros((lane - edge, lane), bf16)
    before = nearest(1, near_ref, far_ref, slice(last_a, first_d))
    before = jnp.where(lax.axis_index("tm") > 0, before, jnp.zeros_like(before))
    after = nearest(0, near_ref, far_ref, slice(first_a, last_a))
    ext_ref[:, :lane] = jnp.concatenate([blank, before], axis=0).T
    ext_ref[:, lane + frames :] = jnp.concatenate([after, blank], axis=0).T

    def chunk(i, carry):
        at = pl.multiple_of(i * rows, rows)
        fetch(i).wait()
        block = ext_ref[pl.ds(at, rows), :]
        for a in range(steps):
            by = lane - (group - 1) - group * a
            stack_ref[pl.ds(pl.multiple_of(a * motifs + at, rows), rows), :] = moved(block, by)[:, :width]
        return carry

    lax.fori_loop(0, motifs // rows, chunk, 0)


def by_lag(w_ref, pack_ref):
    lags = w_ref.shape[0]
    steps = lags // group
    rows = [jnp.concatenate([w_ref[group * a + b] for a in range(steps)], axis=1) for b in range(group)]
    few = first_a // steps
    rows.append(jnp.concatenate([pack_ref[few * a : few * (a + 1), :] for a in range(steps)], axis=1))
    return jnp.concatenate(rows, axis=0)


def forward_half(stack_ref, w0_ref, w1_ref, p0_ref, p1_ref, out_ref):
    mine = lax.axis_index("tm")
    span = stack_ref.shape[0] // 4
    left = jnp.concatenate([by_lag(w0_ref, p0_ref), by_lag(w1_ref, p1_ref)], axis=1)
    starts = [pl.multiple_of((mine ^ p) * span, span) for p in (0, 1)]
    for at, size in tiles(out_ref.shape[1], 256):
        cols = slice(at, at + size)
        right = jnp.concatenate([stack_ref[pl.ds(start, span), cols] for start in starts], axis=0)
        out_ref[:, cols] = jnp.dot(left, right, preferred_element_type=f32)


def forward_backward(scale, frames, *refs):
    base_ref, stack_ref, data_ref, behav_ref = refs[:4]
    w_parts, packs = refs[4:8], refs[8:12]
    grad_refs, resid_ref = refs[12:16], refs[16]
    late_ref, v_ref, out_ref, back_ref, few_ref, turn_ref, sum_ref = refs[17:]
    part, neurons, motifs = w_parts[0].shape
    lags = 4 * part
    features = v_ref.shape[0] // lags
    steps = lags // group
    width = frames + lane
    mine = lax.axis_index("tm")
    _, y = place()
    valid = mine < 3
    parts = list(tiles(width, 256))

    def reach(at, size):
        return slice(at, min(at + size + lane, width))

    left = jnp.concatenate([by_lag(w, p) for w, p in zip(w_parts[2:], packs[2:])], axis=1)
    span = stack_ref.shape[0] // 4
    starts = [pl.multiple_of((mine ^ p) * span, span) for p in (2, 3)]
    after = nearest(0, packs[1], packs[3], slice(first_d, first_b))
    after = jnp.concatenate([after, jnp.zeros((lane - edge, lane), bf16)], axis=0).T
    after_few = nearest(0, packs[1], packs[3], slice(first_b, pack_rows))

    def product(at, size):
        cols = slice(at, at + size)
        right = jnp.concatenate([stack_ref[pl.ds(start, span), cols] for start in starts], axis=0)
        out_ref[:, cols] = jnp.dot(left, right, preferred_element_type=f32) + base_ref[:, cols]

    def recon(first, count, at, size):
        total = None
        for b in range(group):
            rows = slice(first + b * count, first + (b + 1) * count)
            term = moved(out_ref[rows, reach(at, size)], group - 1 - b)[:, :size]
            total = term if total is None else total + term
        return scale * total

    def residual(at, size):
        cols = slice(at, at + size)
        past = at >= frames
        own = after if past else data_ref[:, cols]
        own_few = after_few if past else behav_ref[:, cols]
        resid = own.astype(f32) - recon(0, neurons, at, size)
        few = behaviour_weight * (own_few.astype(f32) - recon(group * neurons, features, at, size))
        if past:
            resid, few = jnp.where(valid, resid, 0.0), jnp.where(valid, few, 0.0)
        resid_ref[:neurons, cols] = resid.astype(bf16)
        resid_ref[neurons:, cols] = few.astype(bf16)

    def spread(at, size):
        block = resid_ref[:neurons, reach(at, size)]
        for a in range(steps):
            back_ref[a * neurons : (a + 1) * neurons, at : at + size] = moved(block, group * a)[:, :size]

    for i, (at, size) in enumerate(parts):
        product(at, size)
        if i == 0:
            for p in range(4):
                v_ref[pl.ds(pl.multiple_of((mine ^ p) * first_a, first_a), first_a)] = packs[p][:first_a, :]
                for a in range(part // group):
                    column = pl.multiple_of((mine ^ p) * span + a * neurons, neurons)
                    for b in range(group):
                        turn_ref[b * motifs : (b + 1) * motifs, pl.ds(column, neurons)] = w_parts[p][group * a + b].T
        if i >= 1:
            residual(*parts[i - 1])
        if i >= 2:
            spread(*parts[i - 2])
    residual(*parts[-1])
    spread(*parts[-2])
    spread(*parts[-1])

    few = resid_ref[neurons:, :].astype(f32)
    for l in range(0, lags, 2):
        pair = jnp.concatenate([moved(few, l)[:, :frames], moved(few, l + 1)[:, :frames]], axis=0)
        few_ref[l * features : (l + 2) * features, :] = pair.astype(bf16)
    v_left = v_ref[...].T

    def gradient(at, size):
        total = jnp.dot(v_left, few_ref[:, at : at + size], preferred_element_type=f32)
        for b in range(group):
            term = late_ref[b * motifs : (b + 1) * motifs, reach(at, size)]
            total = total + moved(term, b)[:, :size]
        for i in range(motifs // patch):
            for j in range(size // lane):
                sum_ref[i * (frames // lane) + at // lane + j] = total[
                    patch * i : patch * (i + 1), lane * j : lane * (j + 1)
                ]

    for i, (at, size) in enumerate(parts):
        cols = slice(at, at + size)
        late_ref[:, cols] = jnp.dot(turn_ref[...], back_ref[:, cols], preferred_element_type=f32)
        if i >= 1:
            gradient(*parts[i - 1])
    for r in range(wide):
        peer = (y + r) % wide
        grad_refs[r][...] = sum_ref[pl.ds(peer * deep, deep)].astype(grad_refs[r].dtype)


def motif_gradients(frames, motifs, stack_ref, resid_ref, keep_ref, relay_ref, send_ref, left_ref):
    out_refs = (keep_ref, send_ref.at[0], relay_ref, send_ref.at[1])
    features = keep_ref.shape[1] - 128
    neurons = resid_ref.shape[0] - features
    steps = stack_ref.shape[0] // motifs
    width = frames + lane
    rows = 16
    mask = lax.broadcasted_iota(jnp.int32, (rows, width), 1) < frames

    def chunk(i, carry):
        at = pl.multiple_of(i * rows, rows)
        block = jnp.where(mask, resid_ref[pl.ds(at, rows), :].astype(f32), 0.0)
        for b in range(group):
            shifted = moved(block, b - (group - 1)).astype(bf16)
            left_ref[pl.ds(pl.multiple_of(b * neurons + at, rows), rows), :] = shifted
        return carry

    lax.fori_loop(0, neurons // rows, chunk, 0)
    block = jnp.where(mask[:features], resid_ref[neurons:, :].astype(f32), 0.0)
    left_ref[group * neurons :, :] = jnp.concatenate(
        [moved(block, b - (group - 1)) for b in range(group)], axis=0
    ).astype(bf16)
    mine = lax.axis_index("tm")
    span = steps * motifs // 4
    for p in (3, 1, 2, 0):
        first = pl.multiple_of((mine ^ p) * span, span)
        result = lax.dot_general(
            left_ref[...], stack_ref[pl.ds(first, span), :], (((1,), (1,)), ((), ())), preferred_element_type=f32
        )
        for a in range(span // motifs):
            for b in range(group):
                target = out_refs[p]
                l = group * a + b
                cols = slice(a * motifs, (a + 1) * motifs)
                few = group * neurons + b * features
                target[l, :neurons, :] = result[b * neurons : (b + 1) * neurons, cols].astype(target.dtype)
                target[l, neurons:, :] = result[few : few + features, cols].astype(target.dtype)


def update_motifs(factor, w_ref, v_ref, keep_ref, got_ref, far_ref, w_out_ref, v_out_ref):
    neurons = w_ref.shape[1]
    lags = w_ref.shape[0]

    def one(l, carry):
        common = far_ref[lags].astype(f32) + far_ref[lags + 1].astype(f32)
        total = keep_ref[l] + got_ref[0, l] + (far_ref[l].astype(f32) + common)
        w_out_ref[l] = jnp.maximum(w_ref[l].astype(f32) + factor * total[:neurons], 0.0).astype(bf16)
        v_out_ref[l] = jnp.maximum(v_ref[l].astype(f32) + factor * total[neurons:], 0.0).astype(bf16)
        return carry

    lax.fori_loop(0, lags, one, 0)


def relay_motifs(relay_ref, got_ref, far_ref):
    lags, rows, _ = relay_ref.shape
    for at, size in tiles(rows, 16):
        part = slice(at, at + size)
        total = relay_ref[:, part, :] + got_ref[1, :, part, :]
        mean = jnp.sum(total, axis=0) * (1.0 / lags)
        high = mean.astype(bf16)
        low = (mean - high.astype(f32)).astype(bf16)
        common = high.astype(f32) + low.astype(f32)
        for l in range(lags):
            far_ref[l, part, :] = (total[l] - common).astype(bf16)
        far_ref[lags, part, :] = high
        far_ref[lags + 1, part, :] = low


def sum_around(*refs):
    parts, out_ref = refs[:wide], refs[wide]
    total = parts[0][...]
    for part in parts[1:]:
        total = total + part[...].astype(f32)
    out_ref[...] = total.astype(out_ref.dtype)


def update(factor, active_hbm, parts_ref, relay_ref, got_ref, out_ref, far_ref, own_ref, sem):
    i, y = place()
    rows = pl.ds(pl.multiple_of(y * patch, patch), patch)
    copy = pltpu.make_async_copy(active_hbm.at[rows, pl.ds(pl.multiple_of(i * lane, lane), lane)], own_ref, sem)
    copy.start()
    total = jnp.sum(parts_ref[...].astype(f32), axis=0)
    copy.wait()
    block = jnp.maximum(own_ref[...].astype(f32) + factor * total, 0.0).astype(bf16)
    for j in range(deep):
        out_ref[j] = block
    relay_motifs(relay_ref, got_ref, far_ref)


def join_columns(parts_ref, out_ref):
    for j in range(deep):
        out_ref[:, lane * j : lane * (j + 1)] = parts_ref[j]


def join_rows(*refs):
    parts, out_ref = refs[:wide], refs[wide]
    _, y = place()
    for r in range(wide):
        row = pl.multiple_of((y + wide - r) % wide * patch, patch)
        out_ref[pl.ds(row, patch), :] = parts[r][...]


def call(body, out_shape, scratch, args, flops=0, moves=1 << 20, vmem=8, in_specs=None):
    if in_specs:
        args = [pltpu.with_memory_space_constraint(a, pltpu.HBM) if p is HBM else a for a, p in zip(args, in_specs)]
    return pl.pallas_call(
        body,
        out_shape=out_shape,
        in_specs=in_specs or [VMEM] * len(args),
        out_specs=jax.tree.map(lambda _: VMEM, out_shape),
        scratch_shapes=scratch,
        compiler_params=pltpu.CompilerParams(vmem_limit_bytes=vmem << 20),
        cost_estimate=pl.CostEstimate(flops=flops, bytes_accessed=moves, transcendentals=0),
    )(*args)


def local(data, behaviour, motifs, behav_motifs, activations):
    lags_here, neurons, width = motifs.shape
    features = behaviour.shape[0]
    frames = activations.shape[1]
    lags = lags_here * lax.axis_size("tm")
    all_frames = frames * lax.axis_size("tm")
    all_neurons = neurons * lax.axis_size("neuron")
    all_features = features * lax.axis_size("neuron")
    scale = 1.0 / (lags * width)
    rate_motif = 0.5 * lags * width / math.sqrt(all_frames)
    rate_active = 0.5 * lags * width / math.sqrt(lags * (all_neurons + 4 * all_features))
    shape = jax.ShapeDtypeStruct
    steps = lags // group

    w2 = crossed(motifs, 2)
    p0 = call(
        pack,
        shape((pack_rows, width), bf16),
        [
            pltpu.VMEM(behav_motifs.shape, bf16),
            pltpu.VMEM((width, lane), bf16),
            pltpu.VMEM((width, lane), bf16),
            pltpu.VMEM((neurons, lane), bf16),
            pltpu.VMEM((features, lane), bf16),
            pltpu.SemaphoreType.DMA((5,)),
        ],
        [behav_motifs, activations, data, behaviour],
        in_specs=[HBM] * 4,
    )
    p2 = crossed(p0, 2)
    p1 = crossed(p0, 1)
    w1 = crossed(motifs, 1)
    p3 = crossed(p2, 1)
    stack = call(
        shift_activations,
        shape((steps * width, frames + lane), bf16),
        [pltpu.VMEM((width, frames + 2 * lane), bf16), pltpu.SemaphoreType.DMA((width // 16,))],
        [p1, p3, activations],
        in_specs=[VMEM, VMEM, HBM],
        moves=8 << 20,
        vmem=8,
    )
    w3 = crossed(w2, 1)
    half = call(
        forward_half,
        shape((group * (neurons + features), frames + lane), f32),
        [],
        [stack, motifs, w1, p0, p1],
        flops=lags * (neurons + features) * width * frames,
        moves=8 << 20,
        vmem=8,
    )

    grads_and_more = call(
        functools.partial(forward_backward, scale, frames),
        [shape((deep, patch, lane), f32 if r == 0 else bf16) for r in range(wide)]
        + [shape((neurons + features, frames + lane), bf16)],
        [
            pltpu.VMEM((group * width, frames + lane), f32),
            pltpu.VMEM((lags * features, width), bf16),
            pltpu.VMEM((group * (neurons + features), frames + lane), f32),
            pltpu.VMEM((steps * neurons, frames + lane), bf16),
            pltpu.VMEM((lags * features, frames), bf16),
            pltpu.VMEM((group * width, steps * neurons), bf16),
            pltpu.VMEM((deep * wide, patch, lane), f32),
        ],
        [half, stack, data, behaviour, motifs, w1, w2, w3, p0, p1, p2, p3],
        flops=3 * lags * (neurons + features) * width * frames,
        moves=4 << 20,
        vmem=24,
    )
    grads, resid = grads_and_more[:wide], grads_and_more[wide]
    around_parts = [grads[0]]
    for r in range(1, wide):
        around_parts.append(around(grads[r], r))

    per_lag = (lags_here, neurons + features, width)
    keep, relay, send = call(
        functools.partial(motif_gradients, frames, width),
        [shape(per_lag, f32), shape(per_lag, f32), shape((2,) + per_lag, f32)],
        [pltpu.VMEM((group * (neurons + features), frames + lane), bf16)],
        [stack, resid],
        flops=2 * lags * (neurons + features) * width * frames,
        moves=4 << 20,
        vmem=8,
    )
    got = crossed(send, 1)

    sums = call(sum_around, shape((deep, patch, lane), bf16), [], around_parts)
    blocks, far = call(
        functools.partial(update, rate_active * scale),
        [shape((deep, patch, lane), bf16), shape((lags_here + 2,) + per_lag[1:], bf16)],
        [pltpu.VMEM((patch, lane), bf16), pltpu.SemaphoreType.DMA],
        [activations, exchanged(sums), relay, got],
        in_specs=[HBM, VMEM, VMEM, VMEM],
    )
    far = crossed(far, 2)
    strip = call(join_columns, shape((patch, frames), bf16), [], [exchanged(blocks)])
    rows = [strip]
    for r in range(1, wide):
        rows.append(around(strip, r))
    new_motifs, new_behav = call(
        functools.partial(update_motifs, rate_motif * scale),
        [shape(motifs.shape, bf16), shape(behav_motifs.shape, bf16)],
        [],
        [motifs, behav_motifs, keep, got, far],
        moves=4 << 20,
    )
    new_active = call(join_rows, shape((width, frames), bf16), [], rows)
    return (new_motifs, new_behav, new_active)


def solution(mesh):
    placed = (
        P("neuron", "tm"),
        P("neuron", "tm"),
        P("tm", "neuron", None),
        P("tm", "neuron", None),
        P(None, "tm"),
    )
    return jax.shard_map(
        local,
        mesh=mesh,
        in_specs=placed,
        out_specs=(P("tm", "neuron", None), P("tm", "neuron", None), P(None, "tm")),
        check_vma=False,
    )
```

```python
import functools
import math

import jax
import jax.numpy as jnp
from jax import lax
from jax.experimental import pallas as pl
from jax.experimental.pallas import tpu as pltpu
from jax.sharding import PartitionSpec as P


behaviour_weight = 2.0
lane = 128
group = 4
deep, wide = 16, 4
coarse_step = 1024
patch = 32
f32 = jnp.float32
bf16 = jnp.bfloat16
VMEM = pl.BlockSpec(memory_space=pltpu.VMEM)
HBM = pl.BlockSpec(memory_space=pltpu.HBM)


def crossed(shard, mask):
    return lax.ppermute(shard, "tm", [(i, i ^ mask) for i in range(4)])


def around(shard, by):
    pairs = [(i * wide + y, i * wide + (y + by) % wide) for i in range(deep) for y in range(wide)]
    return lax.ppermute(shard, "neuron", pairs)


def exchanged(blocks):
    groups = [[i * wide + y for i in range(deep)] for y in range(wide)]
    return lax.all_to_all(blocks, "neuron", 0, 0, axis_index_groups=groups, tiled=True)


def place():
    me = lax.axis_index("neuron")
    return me // wide, me % wide


def moved(x, by):
    by = by % x.shape[1]
    return x if by == 0 else pltpu.roll(x, x.shape[1] - by, 1)


def tiles(width, step):
    at = 0
    while at < width:
        size = min(step, width - at)
        yield at, size
        at += size


edge = 32
first_a, last_a, first_d, first_b = 64, 96, 128, 160
pack_rows = 168


def fetched(pairs, sems):
    copies = [pltpu.make_async_copy(source, target, sems.at[i]) for i, (source, target) in enumerate(pairs)]
    for copy in copies:
        copy.start()
    for copy in copies:
        copy.wait()


def pack(v_hbm, active_hbm, data_hbm, behav_hbm, out_ref, v_ref, head_ref, tail_ref, data_ref, behav_ref, sems):
    frames = active_hbm.shape[1]
    fetched(
        [
            (v_hbm, v_ref),
            (active_hbm.at[:, :lane], head_ref),
            (active_hbm.at[:, frames - lane :], tail_ref),
            (data_hbm.at[:, :lane], data_ref),
            (behav_hbm.at[:, :lane], behav_ref),
        ],
        sems,
    )
    out_ref[:first_a] = v_ref[...].reshape(first_a, lane)
    out_ref[first_a:last_a] = head_ref[...].T[:edge]
    out_ref[last_a:first_d] = tail_ref[...].T[lane - edge :]
    out_ref[first_d:first_b] = data_ref[...].T[:edge]
    out_ref[first_b:] = behav_ref[...]


def nearest(odd, near_ref, far_ref, rows):
    mine = lax.axis_index("tm")
    return jnp.where(mine % 2 == odd, near_ref[rows, :], far_ref[rows, :])


def shift_activations(near_ref, far_ref, active_hbm, stack_ref, ext_ref, sems):
    motifs, frames = active_hbm.shape
    width = stack_ref.shape[1]
    steps = stack_ref.shape[0] // motifs
    rows = 16

    def fetch(i):
        part = pl.ds(pl.multiple_of(i * rows, rows), rows)
        return pltpu.make_async_copy(active_hbm.at[part], ext_ref.at[part, lane : lane + frames], sems.at[i])

    for i in range(motifs // rows):
        fetch(i).start()
    blank = jnp.zeros((lane - edge, lane), bf16)
    before = nearest(1, near_ref, far_ref, slice(last_a, first_d))
    before = jnp.where(lax.axis_index("tm") > 0, before, jnp.zeros_like(before))
    after = nearest(0, near_ref, far_ref, slice(first_a, last_a))
    ext_ref[:, :lane] = jnp.concatenate([blank, before], axis=0).T
    ext_ref[:, lane + frames :] = jnp.concatenate([after, blank], axis=0).T

    def chunk(i, carry):
        at = pl.multiple_of(i * rows, rows)
        fetch(i).wait()
        block = ext_ref[pl.ds(at, rows), :]
        for a in range(steps):
            by = lane - (group - 1) - group * a
            stack_ref[pl.ds(pl.multiple_of(a * motifs + at, rows), rows), :] = moved(block, by)[:, :width]
        return carry

    lax.fori_loop(0, motifs // rows, chunk, 0)


def by_lag(w_ref, pack_ref):
    lags = w_ref.shape[0]
    steps = lags // group
    rows = [jnp.concatenate([w_ref[group * a + b] for a in range(steps)], axis=1) for b in range(group)]
    few = first_a // steps
    rows.append(jnp.concatenate([pack_ref[few * a : few * (a + 1), :] for a in range(steps)], axis=1))
    return jnp.concatenate(rows, axis=0)


def forward_half(stack_ref, w0_ref, w1_ref, p0_ref, p1_ref, out_ref, turned_ref):
    mine = lax.axis_index("tm")
    span = stack_ref.shape[0] // 4
    left = jnp.concatenate([by_lag(w0_ref, p0_ref), by_lag(w1_ref, p1_ref)], axis=1)
    starts = [pl.multiple_of((mine ^ p) * span, span) for p in (0, 1)]
    for at, size in tiles(out_ref.shape[1], 256):
        cols = slice(at, at + size)
        right = jnp.concatenate([stack_ref[pl.ds(start, span), cols] for start in starts], axis=0)
        out_ref[:, cols] = jnp.dot(left, right, preferred_element_type=f32)
        if at == 0:
            _, neurons, motifs = w0_ref.shape
            for p, w_ref in enumerate((w0_ref, w1_ref)):
                for a in range(span // motifs):
                    first = p * span + a * neurons
                    for b in range(group):
                        turned_ref[b * motifs : (b + 1) * motifs, first : first + neurons] = w_ref[group * a + b].T


def forward_backward(scale, frames, *refs):
    base_ref, turned_ref, stack_ref, data_ref, behav_ref = refs[:5]
    w_parts, packs = refs[5:9], refs[9:13]
    grad_refs, resid_ref = refs[13:17], refs[17]
    late_ref, v_ref, out_ref, back_ref, few_ref, turn_ref, sum_ref = refs[18:]
    part, neurons, motifs = w_parts[0].shape
    lags = 4 * part
    features = v_ref.shape[0] // lags
    steps = lags // group
    width = frames + lane
    mine = lax.axis_index("tm")
    _, y = place()
    valid = mine < 3
    parts = list(tiles(width, 256))

    def reach(at, size):
        return slice(at, min(at + size + lane, width))

    left = jnp.concatenate([by_lag(w, p) for w, p in zip(w_parts[2:], packs[2:])], axis=1)
    span = stack_ref.shape[0] // 4
    starts = [pl.multiple_of((mine ^ p) * span, span) for p in (2, 3)]
    after = nearest(0, packs[1], packs[3], slice(first_d, first_b))
    after = jnp.concatenate([after, jnp.zeros((lane - edge, lane), bf16)], axis=0).T
    after_few = nearest(0, packs[1], packs[3], slice(first_b, pack_rows))

    def product(at, size):
        cols = slice(at, at + size)
        right = jnp.concatenate([stack_ref[pl.ds(start, span), cols] for start in starts], axis=0)
        out_ref[:, cols] = jnp.dot(left, right, preferred_element_type=f32) + base_ref[:, cols]

    def recon(first, count, at, size):
        total = None
        for b in range(group):
            rows = slice(first + b * count, first + (b + 1) * count)
            term = moved(out_ref[rows, reach(at, size)], group - 1 - b)[:, :size]
            total = term if total is None else total + term
        return scale * total

    def residual(at, size):
        cols = slice(at, at + size)
        past = at >= frames
        own = after if past else data_ref[:, cols]
        own_few = after_few if past else behav_ref[:, cols]
        resid = own.astype(f32) - recon(0, neurons, at, size)
        few = behaviour_weight * (own_few.astype(f32) - recon(group * neurons, features, at, size))
        if past:
            resid, few = jnp.where(valid, resid, 0.0), jnp.where(valid, few, 0.0)
        resid_ref[:neurons, cols] = resid.astype(bf16)
        resid_ref[neurons:, cols] = few.astype(bf16)

    def spread(at, size):
        block = resid_ref[:neurons, reach(at, size)]
        for a in range(steps):
            back_ref[a * neurons : (a + 1) * neurons, at : at + size] = moved(block, group * a)[:, :size]

    done = []
    coarse = list(tiles(width, coarse_step))
    for i, (at, size) in enumerate(parts):
        product(at, size)
        if i == 0:
            for p in range(4):
                v_ref[pl.ds(pl.multiple_of((mine ^ p) * first_a, first_a), first_a)] = packs[p][:first_a, :]
                for a in range(part // group):
                    column = pl.multiple_of((mine ^ p) * span + a * neurons, neurons)
                    for b in range(group):
                        if p < 2:
                            turned = turned_ref[
                                b * motifs : (b + 1) * motifs, p * span + a * neurons : p * span + (a + 1) * neurons
                            ]
                        else:
                            turned = w_parts[p][group * a + b].T
                        turn_ref[b * motifs : (b + 1) * motifs, pl.ds(column, neurons)] = turned
        while len(done) < len(coarse) and (
            reach(*coarse[len(done)]).stop <= at + size
        ):
            residual(*coarse[len(done)])
            if done:
                spread(*coarse[len(done) - 1])
            done.append(at)
    spread(*coarse[-1])

    few = resid_ref[neurons:, :].astype(f32)
    for l in range(0, lags, 2):
        pair = jnp.concatenate([moved(few, l)[:, :frames], moved(few, l + 1)[:, :frames]], axis=0)
        few_ref[l * features : (l + 2) * features, :] = pair.astype(bf16)
    v_left = v_ref[...].T

    def gradient(at, size):
        total = jnp.dot(v_left, few_ref[:, at : at + size], preferred_element_type=f32)
        for b in range(group):
            term = late_ref[b * motifs : (b + 1) * motifs, reach(at, size)]
            total = total + moved(term, b)[:, :size]
        for i in range(motifs // patch):
            for j in range(size // lane):
                sum_ref[i * (frames // lane) + at // lane + j] = total[
                    patch * i : patch * (i + 1), lane * j : lane * (j + 1)
                ]

    waiting = list(tiles(frames, coarse_step))
    for at, size in parts:
        cols = slice(at, at + size)
        late_ref[:, cols] = jnp.dot(turn_ref[...], back_ref[:, cols], preferred_element_type=f32)
        while waiting and reach(*waiting[0]).stop <= at + size:
            gradient(*waiting.pop(0))
    for r in range(wide):
        peer = (y + r) % wide
        grad_refs[r][...] = sum_ref[pl.ds(peer * deep, deep)].astype(grad_refs[r].dtype)


def motif_gradients(frames, motifs, stack_ref, resid_ref, keep_ref, relay_ref, send_ref, left_ref):
    out_refs = (keep_ref, send_ref.at[0], relay_ref, send_ref.at[1])
    features = keep_ref.shape[1] - 128
    neurons = resid_ref.shape[0] - features
    steps = stack_ref.shape[0] // motifs
    width = frames + lane
    rows = 16
    mask = lax.broadcasted_iota(jnp.int32, (rows, width), 1) < frames

    def chunk(i, carry):
        at = pl.multiple_of(i * rows, rows)
        block = jnp.where(mask, resid_ref[pl.ds(at, rows), :].astype(f32), 0.0)
        for b in range(group):
            shifted = moved(block, b - (group - 1)).astype(bf16)
            left_ref[pl.ds(pl.multiple_of(b * neurons + at, rows), rows), :] = shifted
        return carry

    lax.fori_loop(0, neurons // rows, chunk, 0)
    block = jnp.where(mask[:features], resid_ref[neurons:, :].astype(f32), 0.0)
    left_ref[group * neurons :, :] = jnp.concatenate(
        [moved(block, b - (group - 1)) for b in range(group)], axis=0
    ).astype(bf16)
    mine = lax.axis_index("tm")
    span = steps * motifs // 4
    for p in (3, 1, 2, 0):
        first = pl.multiple_of((mine ^ p) * span, span)
        result = lax.dot_general(
            left_ref[...], stack_ref[pl.ds(first, span), :], (((1,), (1,)), ((), ())), preferred_element_type=f32
        )
        for a in range(span // motifs):
            for b in range(group):
                target = out_refs[p]
                l = group * a + b
                cols = slice(a * motifs, (a + 1) * motifs)
                few = group * neurons + b * features
                target[l, :neurons, :] = result[b * neurons : (b + 1) * neurons, cols].astype(target.dtype)
                target[l, neurons:, :] = result[few : few + features, cols].astype(target.dtype)


def update_motifs(factor, w_ref, v_ref, keep_ref, got_ref, far_ref, w_out_ref, v_out_ref):
    neurons = w_ref.shape[1]
    lags = w_ref.shape[0]

    def one(l, carry):
        common = far_ref[lags].astype(f32) + far_ref[lags + 1].astype(f32)
        total = keep_ref[l] + got_ref[0, l] + (far_ref[l].astype(f32) + common)
        w_out_ref[l] = jnp.maximum(w_ref[l].astype(f32) + factor * total[:neurons], 0.0).astype(bf16)
        v_out_ref[l] = jnp.maximum(v_ref[l].astype(f32) + factor * total[neurons:], 0.0).astype(bf16)
        return carry

    lax.fori_loop(0, lags, one, 0)


def relay_motifs(relay_ref, got_ref, far_ref):
    lags, rows, _ = relay_ref.shape
    for at, size in tiles(rows, 16):
        part = slice(at, at + size)
        total = relay_ref[:, part, :] + got_ref[1, :, part, :]
        mean = jnp.sum(total, axis=0) * (1.0 / lags)
        high = mean.astype(bf16)
        low = (mean - high.astype(f32)).astype(bf16)
        common = high.astype(f32) + low.astype(f32)
        for l in range(lags):
            far_ref[l, part, :] = (total[l] - common).astype(bf16)
        far_ref[lags, part, :] = high
        far_ref[lags + 1, part, :] = low


def sum_around(*refs):
    parts, out_ref = refs[:wide], refs[wide]
    total = parts[0][...]
    for part in parts[1:]:
        total = total + part[...].astype(f32)
    out_ref[...] = total.astype(out_ref.dtype)


def update(factor, active_hbm, parts_ref, out_ref, own_ref, sem):
    i, y = place()
    rows = pl.ds(pl.multiple_of(y * patch, patch), patch)
    copy = pltpu.make_async_copy(active_hbm.at[rows, pl.ds(pl.multiple_of(i * lane, lane), lane)], own_ref, sem)
    copy.start()
    total = jnp.sum(parts_ref[...].astype(f32), axis=0)
    copy.wait()
    block = jnp.maximum(own_ref[...].astype(f32) + factor * total, 0.0).astype(bf16)
    for j in range(deep):
        out_ref[j] = block


def join_columns(parts_ref, out_ref):
    for j in range(deep):
        out_ref[:, lane * j : lane * (j + 1)] = parts_ref[j]


def join_rows(*refs):
    parts, out_ref = refs[:wide], refs[wide]
    _, y = place()
    for r in range(wide):
        row = pl.multiple_of((y + wide - r) % wide * patch, patch)
        out_ref[pl.ds(row, patch), :] = parts[r][...]


def call(body, out_shape, scratch, args, flops=0, moves=1 << 20, vmem=8, in_specs=None):
    if in_specs:
        args = [pltpu.with_memory_space_constraint(a, pltpu.HBM) if p is HBM else a for a, p in zip(args, in_specs)]
    return pl.pallas_call(
        body,
        out_shape=out_shape,
        in_specs=in_specs or [VMEM] * len(args),
        out_specs=jax.tree.map(lambda _: VMEM, out_shape),
        scratch_shapes=scratch,
        compiler_params=pltpu.CompilerParams(vmem_limit_bytes=vmem << 20),
        cost_estimate=pl.CostEstimate(flops=flops, bytes_accessed=moves, transcendentals=0),
    )(*args)


def local(data, behaviour, motifs, behav_motifs, activations):
    lags_here, neurons, width = motifs.shape
    features = behaviour.shape[0]
    frames = activations.shape[1]
    lags = lags_here * lax.axis_size("tm")
    all_frames = frames * lax.axis_size("tm")
    all_neurons = neurons * lax.axis_size("neuron")
    all_features = features * lax.axis_size("neuron")
    scale = 1.0 / (lags * width)
    rate_motif = 0.5 * lags * width / math.sqrt(all_frames)
    rate_active = 0.5 * lags * width / math.sqrt(lags * (all_neurons + 4 * all_features))
    shape = jax.ShapeDtypeStruct
    steps = lags // group

    w2 = crossed(motifs, 2)
    p0 = call(
        pack,
        shape((pack_rows, width), bf16),
        [
            pltpu.VMEM(behav_motifs.shape, bf16),
            pltpu.VMEM((width, lane), bf16),
            pltpu.VMEM((width, lane), bf16),
            pltpu.VMEM((neurons, lane), bf16),
            pltpu.VMEM((features, lane), bf16),
            pltpu.SemaphoreType.DMA((5,)),
        ],
        [behav_motifs, activations, data, behaviour],
        in_specs=[HBM] * 4,
    )
    p2 = crossed(p0, 2)
    p1 = crossed(p0, 1)
    w1 = crossed(motifs, 1)
    p3 = crossed(p2, 1)
    stack = call(
        shift_activations,
        shape((steps * width, frames + lane), bf16),
        [pltpu.VMEM((width, frames + 2 * lane), bf16), pltpu.SemaphoreType.DMA((width // 16,))],
        [p1, p3, activations],
        in_specs=[VMEM, VMEM, HBM],
        moves=8 << 20,
        vmem=8,
    )
    w3 = crossed(w2, 1)
    half, turned = call(
        forward_half,
        [shape((group * (neurons + features), frames + lane), f32), shape((group * width, steps // 2 * neurons), bf16)],
        [],
        [stack, motifs, w1, p0, p1],
        flops=lags * (neurons + features) * width * frames,
        moves=8 << 20,
        vmem=8,
    )

    grads_and_more = call(
        functools.partial(forward_backward, scale, frames),
        [shape((deep, patch, lane), f32 if r == 0 else bf16) for r in range(wide)]
        + [shape((neurons + features, frames + lane), bf16)],
        [
            pltpu.VMEM((group * width, frames + lane), f32),
            pltpu.VMEM((lags * features, width), bf16),
            pltpu.VMEM((group * (neurons + features), frames + lane), f32),
            pltpu.VMEM((steps * neurons, frames + lane), bf16),
            pltpu.VMEM((lags * features, frames), bf16),
            pltpu.VMEM((group * width, steps * neurons), bf16),
            pltpu.VMEM((deep * wide, patch, lane), f32),
        ],
        [half, turned, stack, data, behaviour, motifs, w1, w2, w3, p0, p1, p2, p3],
        flops=3 * lags * (neurons + features) * width * frames,
        moves=4 << 20,
        vmem=24,
    )
    grads, resid = grads_and_more[:wide], grads_and_more[wide]
    around_parts = [grads[0]]
    for r in range(1, wide):
        around_parts.append(around(grads[r], r))

    per_lag = (lags_here, neurons + features, width)
    keep, relay, send = call(
        functools.partial(motif_gradients, frames, width),
        [shape(per_lag, f32), shape(per_lag, f32), shape((2,) + per_lag, f32)],
        [pltpu.VMEM((group * (neurons + features), frames + lane), bf16)],
        [stack, resid],
        flops=2 * lags * (neurons + features) * width * frames,
        moves=4 << 20,
        vmem=8,
    )
    got = crossed(send, 1)

    sums = call(sum_around, shape((deep, patch, lane), bf16), [], around_parts)
    blocks = call(
        functools.partial(update, rate_active * scale),
        shape((deep, patch, lane), bf16),
        [pltpu.VMEM((patch, lane), bf16), pltpu.SemaphoreType.DMA],
        [activations, exchanged(sums)],
        in_specs=[HBM, VMEM],
    )
    far = call(
        relay_motifs,
        shape((lags_here + 2,) + per_lag[1:], bf16),
        [],
        [relay, got],
        moves=4 << 20,
    )
    far = crossed(far, 2)
    blocks = exchanged(blocks)
    strip = call(join_columns, shape((patch, frames), bf16), [], [blocks])
    rows = [strip]
    for r in range(1, wide):
        rows.append(around(strip, r))
    new_motifs, new_behav = call(
        functools.partial(update_motifs, rate_motif * scale),
        [shape(motifs.shape, bf16), shape(behav_motifs.shape, bf16)],
        [],
        [motifs, behav_motifs, keep, got, far],
        moves=4 << 20,
    )
    new_active = call(join_rows, shape((width, frames), bf16), [], rows)
    return (new_motifs, new_behav, new_active)


def solution(mesh):
    placed = (
        P("neuron", "tm"),
        P("neuron", "tm"),
        P("tm", "neuron", None),
        P("tm", "neuron", None),
        P(None, "tm"),
    )
    return jax.shard_map(
        local,
        mesh=mesh,
        in_specs=placed,
        out_specs=(P("tm", "neuron", None), P("tm", "neuron", None), P(None, "tm")),
        check_vma=False,
    )
```

```python
import functools
import math

import jax
import jax.numpy as jnp
from jax import lax
from jax.experimental import pallas as pl
from jax.experimental.pallas import tpu as pltpu
from jax.sharding import PartitionSpec as P


behaviour_weight = 2.0
lane = 128
group = 4
deep, wide = 16, 4
coarse_step = 1024
patch = 32
f32 = jnp.float32
bf16 = jnp.bfloat16
VMEM = pl.BlockSpec(memory_space=pltpu.VMEM)
HBM = pl.BlockSpec(memory_space=pltpu.HBM)


def crossed(shard, mask):
    return lax.ppermute(shard, "tm", [(i, i ^ mask) for i in range(4)])


def around(shard, by):
    pairs = [(i * wide + y, i * wide + (y + by) % wide) for i in range(deep) for y in range(wide)]
    return lax.ppermute(shard, "neuron", pairs)


def exchanged(blocks):
    groups = [[i * wide + y for i in range(deep)] for y in range(wide)]
    return lax.all_to_all(blocks, "neuron", 0, 0, axis_index_groups=groups, tiled=True)


def place():
    me = lax.axis_index("neuron")
    return me // wide, me % wide


def moved(x, by):
    by = by % x.shape[1]
    return x if by == 0 else pltpu.roll(x, x.shape[1] - by, 1)


def tiles(width, step):
    at = 0
    while at < width:
        size = min(step, width - at)
        yield at, size
        at += size


edge = 32
first_a, last_a, first_d, first_b = 64, 96, 128, 160
pack_rows = 168


def fetched(pairs, sems):
    copies = [pltpu.make_async_copy(source, target, sems.at[i]) for i, (source, target) in enumerate(pairs)]
    for copy in copies:
        copy.start()
    for copy in copies:
        copy.wait()


def pack(v_hbm, active_hbm, data_hbm, behav_hbm, out_ref, active_ref, v_ref, data_ref, behav_ref, sems):
    frames = active_hbm.shape[1]
    fetched(
        [
            (active_hbm, active_ref),
            (v_hbm, v_ref),
            (data_hbm.at[:, :lane], data_ref),
            (behav_hbm.at[:, :lane], behav_ref),
        ],
        sems,
    )
    out_ref[:first_a] = v_ref[...].reshape(first_a, lane)
    out_ref[first_a:last_a] = active_ref[:, :lane].T[:edge]
    out_ref[last_a:first_d] = active_ref[:, frames - lane :].T[lane - edge :]
    out_ref[first_d:first_b] = data_ref[...].T[:edge]
    out_ref[first_b:] = behav_ref[...]


def nearest(odd, near_ref, far_ref, rows):
    mine = lax.axis_index("tm")
    return jnp.where(mine % 2 == odd, near_ref[rows, :], far_ref[rows, :])


def shift_activations(near_ref, far_ref, active_ref, stack_ref, ext_ref):
    motifs, frames = active_ref.shape
    width = stack_ref.shape[1]
    steps = stack_ref.shape[0] // motifs
    rows = 16
    blank = jnp.zeros((lane - edge, lane), bf16)
    before = nearest(1, near_ref, far_ref, slice(last_a, first_d))
    before = jnp.where(lax.axis_index("tm") > 0, before, jnp.zeros_like(before))
    after = nearest(0, near_ref, far_ref, slice(first_a, last_a))
    ext_ref[:, :lane] = jnp.concatenate([blank, before], axis=0).T
    ext_ref[:, lane : lane + frames] = active_ref[...]
    ext_ref[:, lane + frames :] = jnp.concatenate([after, blank], axis=0).T

    def chunk(i, carry):
        at = pl.multiple_of(i * rows, rows)
        block = ext_ref[pl.ds(at, rows), :]
        for a in range(steps):
            by = lane - (group - 1) - group * a
            stack_ref[pl.ds(pl.multiple_of(a * motifs + at, rows), rows), :] = moved(block, by)[:, :width]
        return carry

    lax.fori_loop(0, motifs // rows, chunk, 0)


def by_lag(w_ref, pack_ref):
    lags = w_ref.shape[0]
    steps = lags // group
    rows = [jnp.concatenate([w_ref[group * a + b] for a in range(steps)], axis=1) for b in range(group)]
    few = first_a // steps
    rows.append(jnp.concatenate([pack_ref[few * a : few * (a + 1), :] for a in range(steps)], axis=1))
    return jnp.concatenate(rows, axis=0)


def forward_half(stack_ref, w0_ref, w1_ref, p0_ref, p1_ref, out_ref, turned_ref):
    mine = lax.axis_index("tm")
    span = stack_ref.shape[0] // 4
    left = jnp.concatenate([by_lag(w0_ref, p0_ref), by_lag(w1_ref, p1_ref)], axis=1)
    starts = [pl.multiple_of((mine ^ p) * span, span) for p in (0, 1)]
    for at, size in tiles(out_ref.shape[1], 256):
        cols = slice(at, at + size)
        right = jnp.concatenate([stack_ref[pl.ds(start, span), cols] for start in starts], axis=0)
        out_ref[:, cols] = jnp.dot(left, right, preferred_element_type=f32)
        if at == 0:
            _, neurons, motifs = w0_ref.shape
            for p, w_ref in enumerate((w0_ref, w1_ref)):
                for a in range(span // motifs):
                    first = p * span + a * neurons
                    for b in range(group):
                        turned_ref[b * motifs : (b + 1) * motifs, first : first + neurons] = w_ref[group * a + b].T


def forward_backward(scale, frames, *refs):
    base_ref, turned_ref, stack_ref, data_ref, behav_ref = refs[:5]
    w_parts, packs = refs[5:9], refs[9:13]
    grad_refs, resid_ref = refs[13:17], refs[17]
    late_ref, v_ref, out_ref, back_ref, few_ref, turn_ref, sum_ref = refs[18:]
    part, neurons, motifs = w_parts[0].shape
    lags = 4 * part
    features = v_ref.shape[0] // lags
    steps = lags // group
    width = frames + lane
    mine = lax.axis_index("tm")
    _, y = place()
    valid = mine < 3
    parts = list(tiles(width, 256))

    def reach(at, size):
        return slice(at, min(at + size + lane, width))

    left = jnp.concatenate([by_lag(w, p) for w, p in zip(w_parts[2:], packs[2:])], axis=1)
    span = stack_ref.shape[0] // 4
    starts = [pl.multiple_of((mine ^ p) * span, span) for p in (2, 3)]
    after = nearest(0, packs[1], packs[3], slice(first_d, first_b))
    after = jnp.concatenate([after, jnp.zeros((lane - edge, lane), bf16)], axis=0).T
    after_few = nearest(0, packs[1], packs[3], slice(first_b, pack_rows))

    def product(at, size):
        cols = slice(at, at + size)
        right = jnp.concatenate([stack_ref[pl.ds(start, span), cols] for start in starts], axis=0)
        out_ref[:, cols] = jnp.dot(left, right, preferred_element_type=f32) + base_ref[:, cols]

    def recon(first, count, at, size):
        total = None
        for b in range(group):
            rows = slice(first + b * count, first + (b + 1) * count)
            term = moved(out_ref[rows, reach(at, size)], group - 1 - b)[:, :size]
            total = term if total is None else total + term
        return scale * total

    def residual(at, size):
        cols = slice(at, at + size)
        past = at >= frames
        own = after if past else data_ref[:, cols]
        own_few = after_few if past else behav_ref[:, cols]
        resid = own.astype(f32) - recon(0, neurons, at, size)
        few = behaviour_weight * (own_few.astype(f32) - recon(group * neurons, features, at, size))
        if past:
            resid, few = jnp.where(valid, resid, 0.0), jnp.where(valid, few, 0.0)
        resid_ref[:neurons, cols] = resid.astype(bf16)
        resid_ref[neurons:, cols] = few.astype(bf16)

    def spread(at, size):
        block = resid_ref[:neurons, reach(at, size)]
        for a in range(steps):
            back_ref[a * neurons : (a + 1) * neurons, at : at + size] = moved(block, group * a)[:, :size]

    done = []
    coarse = list(tiles(width, coarse_step))
    for i, (at, size) in enumerate(parts):
        product(at, size)
        if i == 0:
            for p in range(4):
                v_ref[pl.ds(pl.multiple_of((mine ^ p) * first_a, first_a), first_a)] = packs[p][:first_a, :]
                for a in range(part // group):
                    column = pl.multiple_of((mine ^ p) * span + a * neurons, neurons)
                    for b in range(group):
                        if p < 2:
                            turned = turned_ref[
                                b * motifs : (b + 1) * motifs, p * span + a * neurons : p * span + (a + 1) * neurons
                            ]
                        else:
                            turned = w_parts[p][group * a + b].T
                        turn_ref[b * motifs : (b + 1) * motifs, pl.ds(column, neurons)] = turned
        while len(done) < len(coarse) and (
            reach(*coarse[len(done)]).stop <= at + size
        ):
            residual(*coarse[len(done)])
            if done:
                spread(*coarse[len(done) - 1])
            done.append(at)
    spread(*coarse[-1])

    few = resid_ref[neurons:, :].astype(f32)
    for l in range(0, lags, 2):
        pair = jnp.concatenate([moved(few, l)[:, :frames], moved(few, l + 1)[:, :frames]], axis=0)
        few_ref[l * features : (l + 2) * features, :] = pair.astype(bf16)
    v_left = v_ref[...].T

    def gradient(at, size):
        total = jnp.dot(v_left, few_ref[:, at : at + size], preferred_element_type=f32)
        for b in range(group):
            term = late_ref[b * motifs : (b + 1) * motifs, reach(at, size)]
            total = total + moved(term, b)[:, :size]
        for i in range(motifs // patch):
            for j in range(size // lane):
                sum_ref[i * (frames // lane) + at // lane + j] = total[
                    patch * i : patch * (i + 1), lane * j : lane * (j + 1)
                ]

    waiting = list(tiles(frames, coarse_step))
    for at, size in parts:
        cols = slice(at, at + size)
        late_ref[:, cols] = jnp.dot(turn_ref[...], back_ref[:, cols], preferred_element_type=f32)
        while waiting and reach(*waiting[0]).stop <= at + size:
            gradient(*waiting.pop(0))
    for r in range(wide):
        peer = (y + r) % wide
        grad_refs[r][...] = sum_ref[pl.ds(peer * deep, deep)].astype(grad_refs[r].dtype)


def motif_gradients(frames, motifs, stack_ref, resid_ref, keep_ref, relay_ref, send_ref, left_ref):
    out_refs = (keep_ref, send_ref.at[0], relay_ref, send_ref.at[1])
    features = keep_ref.shape[1] - 128
    neurons = resid_ref.shape[0] - features
    steps = stack_ref.shape[0] // motifs
    width = frames + lane
    rows = 16
    mask = lax.broadcasted_iota(jnp.int32, (rows, width), 1) < frames

    def chunk(i, carry):
        at = pl.multiple_of(i * rows, rows)
        block = jnp.where(mask, resid_ref[pl.ds(at, rows), :].astype(f32), 0.0)
        for b in range(group):
            shifted = moved(block, b - (group - 1)).astype(bf16)
            left_ref[pl.ds(pl.multiple_of(b * neurons + at, rows), rows), :] = shifted
        return carry

    lax.fori_loop(0, neurons // rows, chunk, 0)
    block = jnp.where(mask[:features], resid_ref[neurons:, :].astype(f32), 0.0)
    left_ref[group * neurons :, :] = jnp.concatenate(
        [moved(block, b - (group - 1)) for b in range(group)], axis=0
    ).astype(bf16)
    mine = lax.axis_index("tm")
    span = steps * motifs // 4
    for p in (3, 1, 2, 0):
        first = pl.multiple_of((mine ^ p) * span, span)
        result = lax.dot_general(
            left_ref[...], stack_ref[pl.ds(first, span), :], (((1,), (1,)), ((), ())), preferred_element_type=f32
        )
        for a in range(span // motifs):
            for b in range(group):
                target = out_refs[p]
                l = group * a + b
                cols = slice(a * motifs, (a + 1) * motifs)
                few = group * neurons + b * features
                target[l, :neurons, :] = result[b * neurons : (b + 1) * neurons, cols].astype(target.dtype)
                target[l, neurons:, :] = result[few : few + features, cols].astype(target.dtype)


def update_motifs(factor, w_ref, v_ref, keep_ref, got_ref, far_ref, w_out_ref, v_out_ref):
    neurons = w_ref.shape[1]
    lags = w_ref.shape[0]

    def one(l, carry):
        common = far_ref[lags].astype(f32) + far_ref[lags + 1].astype(f32)
        total = keep_ref[l] + got_ref[0, l] + (far_ref[l].astype(f32) + common)
        w_out_ref[l] = jnp.maximum(w_ref[l].astype(f32) + factor * total[:neurons], 0.0).astype(bf16)
        v_out_ref[l] = jnp.maximum(v_ref[l].astype(f32) + factor * total[neurons:], 0.0).astype(bf16)
        return carry

    lax.fori_loop(0, lags, one, 0)


def relay_motifs(relay_ref, got_ref, far_ref):
    lags, rows, _ = relay_ref.shape
    for at, size in tiles(rows, 16):
        part = slice(at, at + size)
        total = relay_ref[:, part, :] + got_ref[1, :, part, :]
        mean = jnp.sum(total, axis=0) * (1.0 / lags)
        high = mean.astype(bf16)
        low = (mean - high.astype(f32)).astype(bf16)
        common = high.astype(f32) + low.astype(f32)
        for l in range(lags):
            far_ref[l, part, :] = (total[l] - common).astype(bf16)
        far_ref[lags, part, :] = high
        far_ref[lags + 1, part, :] = low


def sum_around(*refs):
    parts, out_ref = refs[:wide], refs[wide]
    total = parts[0][...]
    for part in parts[1:]:
        total = total + part[...].astype(f32)
    out_ref[...] = total.astype(out_ref.dtype)


def update(factor, active_ref, parts_ref, out_ref):
    i, y = place()
    own = active_ref[pl.ds(pl.multiple_of(y * patch, patch), patch), pl.ds(pl.multiple_of(i * lane, lane), lane)]
    total = jnp.sum(parts_ref[...].astype(f32), axis=0)
    block = jnp.maximum(own.astype(f32) + factor * total, 0.0).astype(bf16)
    for j in range(deep):
        out_ref[j] = block


def join_columns(parts_ref, out_ref):
    for j in range(deep):
        out_ref[:, lane * j : lane * (j + 1)] = parts_ref[j]


def join_rows(*refs):
    parts, out_ref = refs[:wide], refs[wide]
    _, y = place()
    for r in range(wide):
        row = pl.multiple_of((y + wide - r) % wide * patch, patch)
        out_ref[pl.ds(row, patch), :] = parts[r][...]


def call(body, out_shape, scratch, args, flops=0, moves=1 << 20, vmem=8, in_specs=None):
    if in_specs:
        args = [pltpu.with_memory_space_constraint(a, pltpu.HBM) if p is HBM else a for a, p in zip(args, in_specs)]
    return pl.pallas_call(
        body,
        out_shape=out_shape,
        in_specs=in_specs or [VMEM] * len(args),
        out_specs=jax.tree.map(lambda _: VMEM, out_shape),
        scratch_shapes=scratch,
        compiler_params=pltpu.CompilerParams(vmem_limit_bytes=vmem << 20),
        cost_estimate=pl.CostEstimate(flops=flops, bytes_accessed=moves, transcendentals=0),
    )(*args)


def local(data, behaviour, motifs, behav_motifs, activations):
    lags_here, neurons, width = motifs.shape
    features = behaviour.shape[0]
    frames = activations.shape[1]
    lags = lags_here * lax.axis_size("tm")
    all_frames = frames * lax.axis_size("tm")
    all_neurons = neurons * lax.axis_size("neuron")
    all_features = features * lax.axis_size("neuron")
    scale = 1.0 / (lags * width)
    rate_motif = 0.5 * lags * width / math.sqrt(all_frames)
    rate_active = 0.5 * lags * width / math.sqrt(lags * (all_neurons + 4 * all_features))
    shape = jax.ShapeDtypeStruct
    steps = lags // group

    w2 = crossed(motifs, 2)
    p0, active = call(
        pack,
        [shape((pack_rows, width), bf16), shape(activations.shape, bf16)],
        [
            pltpu.VMEM(behav_motifs.shape, bf16),
            pltpu.VMEM((neurons, lane), bf16),
            pltpu.VMEM((features, lane), bf16),
            pltpu.SemaphoreType.DMA((4,)),
        ],
        [behav_motifs, activations, data, behaviour],
        in_specs=[HBM] * 4,
    )
    p2 = crossed(p0, 2)
    p1 = crossed(p0, 1)
    w1 = crossed(motifs, 1)
    p3 = crossed(p2, 1)
    stack = call(
        shift_activations,
        shape((steps * width, frames + lane), bf16),
        [pltpu.VMEM((width, frames + 2 * lane), bf16)],
        [p1, p3, active],
        moves=8 << 20,
        vmem=8,
    )
    w3 = crossed(w2, 1)
    half, turned = call(
        forward_half,
        [shape((group * (neurons + features), frames + lane), f32), shape((group * width, steps // 2 * neurons), bf16)],
        [],
        [stack, motifs, w1, p0, p1],
        flops=lags * (neurons + features) * width * frames,
        moves=8 << 20,
        vmem=8,
    )

    grads_and_more = call(
        functools.partial(forward_backward, scale, frames),
        [shape((deep, patch, lane), f32 if r == 0 else bf16) for r in range(wide)]
        + [shape((neurons + features, frames + lane), bf16)],
        [
            pltpu.VMEM((group * width, frames + lane), f32),
            pltpu.VMEM((lags * features, width), bf16),
            pltpu.VMEM((group * (neurons + features), frames + lane), f32),
            pltpu.VMEM((steps * neurons, frames + lane), bf16),
            pltpu.VMEM((lags * features, frames), bf16),
            pltpu.VMEM((group * width, steps * neurons), bf16),
            pltpu.VMEM((deep * wide, patch, lane), f32),
        ],
        [half, turned, stack, data, behaviour, motifs, w1, w2, w3, p0, p1, p2, p3],
        flops=3 * lags * (neurons + features) * width * frames,
        moves=4 << 20,
        vmem=24,
    )
    grads, resid = grads_and_more[:wide], grads_and_more[wide]
    around_parts = [grads[0]]
    for r in range(1, wide):
        around_parts.append(around(grads[r], r))

    per_lag = (lags_here, neurons + features, width)
    keep, relay, send = call(
        functools.partial(motif_gradients, frames, width),
        [shape(per_lag, f32), shape(per_lag, f32), shape((2,) + per_lag, f32)],
        [pltpu.VMEM((group * (neurons + features), frames + lane), bf16)],
        [stack, resid],
        flops=2 * lags * (neurons + features) * width * frames,
        moves=4 << 20,
        vmem=8,
    )
    got = crossed(send, 1)

    sums = call(sum_around, shape((deep, patch, lane), bf16), [], around_parts)
    blocks = call(
        functools.partial(update, rate_active * scale),
        shape((deep, patch, lane), bf16),
        [],
        [active, exchanged(sums)],
    )
    far = call(
        relay_motifs,
        shape((lags_here + 2,) + per_lag[1:], bf16),
        [],
        [relay, got],
        moves=4 << 20,
    )
    far = crossed(far, 2)
    blocks = exchanged(blocks)
    strip = call(join_columns, shape((patch, frames), bf16), [], [blocks])
    rows = [strip]
    for r in range(1, wide):
        rows.append(around(strip, r))
    new_motifs, new_behav = call(
        functools.partial(update_motifs, rate_motif * scale),
        [shape(motifs.shape, bf16), shape(behav_motifs.shape, bf16)],
        [],
        [motifs, behav_motifs, keep, got, far],
        moves=4 << 20,
    )
    new_active = call(join_rows, shape((width, frames), bf16), [], rows)
    return (new_motifs, new_behav, new_active)


def solution(mesh):
    placed = (
        P("neuron", "tm"),
        P("neuron", "tm"),
        P("tm", "neuron", None),
        P("tm", "neuron", None),
        P(None, "tm"),
    )
    return jax.shard_map(
        local,
        mesh=mesh,
        in_specs=placed,
        out_specs=(P("tm", "neuron", None), P("tm", "neuron", None), P(None, "tm")),
        check_vma=False,
    )
```

```python
import functools
import math

import jax
import jax.numpy as jnp
from jax import lax
from jax.experimental import pallas as pl
from jax.experimental.pallas import tpu as pltpu
from jax.sharding import PartitionSpec as P


behaviour_weight = 2.0
lane = 128
group = 4
deep, wide = 16, 4
coarse_step = 1024
patch = 32
f32 = jnp.float32
bf16 = jnp.bfloat16
VMEM = pl.BlockSpec(memory_space=pltpu.VMEM)
HBM = pl.BlockSpec(memory_space=pltpu.HBM)


def crossed(shard, mask):
    return lax.ppermute(shard, "tm", [(i, i ^ mask) for i in range(4)])


def around(shard, by):
    pairs = [(i * wide + y, i * wide + (y + by) % wide) for i in range(deep) for y in range(wide)]
    return lax.ppermute(shard, "neuron", pairs)


def exchanged(blocks):
    groups = [[i * wide + y for i in range(deep)] for y in range(wide)]
    return lax.all_to_all(blocks, "neuron", 0, 0, axis_index_groups=groups, tiled=True)


def place():
    me = lax.axis_index("neuron")
    return me // wide, me % wide


def moved(x, by):
    by = by % x.shape[1]
    return x if by == 0 else pltpu.roll(x, x.shape[1] - by, 1)


def tiles(width, step):
    at = 0
    while at < width:
        size = min(step, width - at)
        yield at, size
        at += size


edge = 32
first_a, last_a, first_d, first_b = 64, 96, 128, 160
pack_rows = 168


def fetched(pairs, sems):
    copies = [pltpu.make_async_copy(source, target, sems.at[i]) for i, (source, target) in enumerate(pairs)]
    for copy in copies:
        copy.start()
    for copy in copies:
        copy.wait()


def pack(v_hbm, active_hbm, data_hbm, behav_hbm, out_ref, active_ref, v_ref, data_ref, behav_ref, sems):
    frames = active_hbm.shape[1]
    fetched(
        [
            (active_hbm, active_ref),
            (v_hbm, v_ref),
            (data_hbm.at[:, :lane], data_ref),
            (behav_hbm.at[:, :lane], behav_ref),
        ],
        sems,
    )
    out_ref[:first_a] = v_ref[...].reshape(first_a, lane)
    out_ref[first_a:last_a] = active_ref[:, :lane].T[:edge]
    out_ref[last_a:first_d] = active_ref[:, frames - lane :].T[lane - edge :]
    out_ref[first_d:first_b] = data_ref[...].T[:edge]
    out_ref[first_b:] = behav_ref[...]


def nearest(odd, near_ref, far_ref, rows):
    mine = lax.axis_index("tm")
    return jnp.where(mine % 2 == odd, near_ref[rows, :], far_ref[rows, :])


def shifted_edges(near_ref, far_ref, active_ref, edge_ref):
    motifs, frames = active_ref.shape
    blank = jnp.zeros((lane - edge, lane), bf16)
    before = nearest(1, near_ref, far_ref, slice(last_a, first_d))
    before = jnp.where(lax.axis_index("tm") > 0, before, jnp.zeros_like(before))
    after = nearest(0, near_ref, far_ref, slice(first_a, last_a))
    first = jnp.concatenate([jnp.concatenate([blank, before], axis=0).T, active_ref[:, :lane]], axis=1)
    last = jnp.concatenate([active_ref[:, frames - lane :], jnp.concatenate([after, blank], axis=0).T], axis=1)
    for a in range(edge_ref.shape[0] // motifs):
        by = lane - (group - 1) - group * a
        edge_ref[a * motifs : (a + 1) * motifs, :lane] = moved(first, by)[:, :lane]
        edge_ref[a * motifs : (a + 1) * motifs, lane:] = moved(last, by)[:, :lane]


def by_lag(w_ref, pack_ref):
    lags = w_ref.shape[0]
    steps = lags // group
    rows = [jnp.concatenate([w_ref[group * a + b] for a in range(steps)], axis=1) for b in range(group)]
    few = first_a // steps
    rows.append(jnp.concatenate([pack_ref[few * a : few * (a + 1), :] for a in range(steps)], axis=1))
    return jnp.concatenate(rows, axis=0)


def forward_half(active_ref, w0_ref, w1_ref, p0_ref, p1_ref, stack_ref, out_ref, turned_ref):
    motifs, frames = active_ref.shape
    rows = 16

    def chunk(i, carry):
        at = pl.multiple_of(i * rows, rows)
        block = active_ref[pl.ds(at, rows), :]
        for a in range(stack_ref.shape[0] // motifs):
            shifted = moved(block, -(group - 1) - group * a)
            stack_ref[pl.ds(pl.multiple_of(a * motifs + at, rows), rows), :] = shifted
        return carry

    lax.fori_loop(0, motifs // rows, chunk, 0)

    mine = lax.axis_index("tm")
    span = stack_ref.shape[0] // 4
    left = jnp.concatenate([by_lag(w0_ref, p0_ref), by_lag(w1_ref, p1_ref)], axis=1)
    starts = [pl.multiple_of((mine ^ p) * span, span) for p in (0, 1)]
    for at, size in list(tiles(frames, 256))[1:]:
        cols = slice(at, at + size)
        right = jnp.concatenate([stack_ref[pl.ds(start, span), cols] for start in starts], axis=0)
        out_ref[:, cols] = jnp.dot(left, right, preferred_element_type=f32)
        if at == 256:
            _, neurons, motifs = w0_ref.shape
            for p, w_ref in enumerate((w0_ref, w1_ref)):
                for a in range(span // motifs):
                    first = p * span + a * neurons
                    for b in range(group):
                        turned_ref[b * motifs : (b + 1) * motifs, first : first + neurons] = w_ref[group * a + b].T


def forward_backward(scale, frames, *refs):
    base_ref, turned_ref, stack_ref, active_ref, data_ref, behav_ref = refs[:6]
    w_parts, packs = refs[6:10], refs[10:14]
    grad_refs, resid_ref, edge_ref = refs[14:18], refs[18], refs[19]
    late_ref, v_ref, out_ref, back_ref, few_ref, turn_ref, sum_ref = refs[20:]
    part, neurons, motifs = w_parts[0].shape
    lags = 4 * part
    features = v_ref.shape[0] // lags
    steps = lags // group
    width = frames + lane
    mine = lax.axis_index("tm")
    _, y = place()
    valid = mine < 3
    parts = list(tiles(width, 256))

    def reach(at, size):
        return slice(at, min(at + size + lane, width))

    shifted_edges(packs[1], packs[3], active_ref, edge_ref)
    lefts = [by_lag(w, p) for w, p in zip(w_parts, packs)]
    span = stack_ref.shape[0] // 4
    starts = [pl.multiple_of((mine ^ p) * span, span) for p in range(4)]
    after = nearest(0, packs[1], packs[3], slice(first_d, first_b))
    after = jnp.concatenate([after, jnp.zeros((lane - edge, lane), bf16)], axis=0).T
    after_few = nearest(0, packs[1], packs[3], slice(first_b, pack_rows))

    def shifted(p, at, size):
        rows = pl.ds(starts[p], span)
        if at == 0:
            return jnp.concatenate([edge_ref[rows, :lane], stack_ref[rows, lane:size]], axis=1)
        return edge_ref[rows, lane:] if at >= frames else stack_ref[rows, at : at + size]

    def product(at, size):
        cols = slice(at, at + size)
        whole = at == 0 or at >= frames
        these = range(4) if whole else (2, 3)
        left = jnp.concatenate([lefts[p] for p in these], axis=1)
        right = jnp.concatenate([shifted(p, at, size) for p in these], axis=0)
        part = jnp.dot(left, right, preferred_element_type=f32)
        out_ref[:, cols] = part if whole else part + base_ref[:, cols]

    def recon(first, count, at, size):
        total = None
        for b in range(group):
            rows = slice(first + b * count, first + (b + 1) * count)
            term = moved(out_ref[rows, reach(at, size)], group - 1 - b)[:, :size]
            total = term if total is None else total + term
        return scale * total

    def residual(at, size):
        cols = slice(at, at + size)
        past = at >= frames
        own = after if past else data_ref[:, cols]
        own_few = after_few if past else behav_ref[:, cols]
        resid = own.astype(f32) - recon(0, neurons, at, size)
        few = behaviour_weight * (own_few.astype(f32) - recon(group * neurons, features, at, size))
        if past:
            resid, few = jnp.where(valid, resid, 0.0), jnp.where(valid, few, 0.0)
        resid_ref[:neurons, cols] = resid.astype(bf16)
        resid_ref[neurons:, cols] = few.astype(bf16)

    def spread(at, size):
        block = resid_ref[:neurons, reach(at, size)]
        for a in range(steps):
            back_ref[a * neurons : (a + 1) * neurons, at : at + size] = moved(block, group * a)[:, :size]

    done = []
    coarse = list(tiles(width, coarse_step))
    for i, (at, size) in enumerate(parts):
        product(at, size)
        if i == 0:
            for p in range(4):
                v_ref[pl.ds(pl.multiple_of((mine ^ p) * first_a, first_a), first_a)] = packs[p][:first_a, :]
                for a in range(part // group):
                    column = pl.multiple_of((mine ^ p) * span + a * neurons, neurons)
                    for b in range(group):
                        if p < 2:
                            turned = turned_ref[
                                b * motifs : (b + 1) * motifs, p * span + a * neurons : p * span + (a + 1) * neurons
                            ]
                        else:
                            turned = w_parts[p][group * a + b].T
                        turn_ref[b * motifs : (b + 1) * motifs, pl.ds(column, neurons)] = turned
        while len(done) < len(coarse) and (
            reach(*coarse[len(done)]).stop <= at + size
        ):
            residual(*coarse[len(done)])
            if done:
                spread(*coarse[len(done) - 1])
            done.append(at)
    spread(*coarse[-1])

    few = resid_ref[neurons:, :].astype(f32)
    for l in range(0, lags, 2):
        pair = jnp.concatenate([moved(few, l)[:, :frames], moved(few, l + 1)[:, :frames]], axis=0)
        few_ref[l * features : (l + 2) * features, :] = pair.astype(bf16)
    v_left = v_ref[...].T

    def gradient(at, size):
        total = jnp.dot(v_left, few_ref[:, at : at + size], preferred_element_type=f32)
        for b in range(group):
            term = late_ref[b * motifs : (b + 1) * motifs, reach(at, size)]
            total = total + moved(term, b)[:, :size]
        for i in range(motifs // patch):
            for j in range(size // lane):
                sum_ref[i * (frames // lane) + at // lane + j] = total[
                    patch * i : patch * (i + 1), lane * j : lane * (j + 1)
                ]

    waiting = list(tiles(frames, coarse_step))
    for at, size in parts:
        cols = slice(at, at + size)
        late_ref[:, cols] = jnp.dot(turn_ref[...], back_ref[:, cols], preferred_element_type=f32)
        while waiting and reach(*waiting[0]).stop <= at + size:
            gradient(*waiting.pop(0))
    for r in range(wide):
        peer = (y + r) % wide
        grad_refs[r][...] = sum_ref[pl.ds(peer * deep, deep)].astype(grad_refs[r].dtype)


def motif_gradients(frames, motifs, stack_ref, edge_ref, resid_ref, keep_ref, relay_ref, send_ref, left_ref):
    out_refs = (keep_ref, send_ref.at[0], relay_ref, send_ref.at[1])
    features = keep_ref.shape[1] - 128
    neurons = resid_ref.shape[0] - features
    steps = stack_ref.shape[0] // motifs
    width = frames + lane
    rows = 16
    mask = lax.broadcasted_iota(jnp.int32, (rows, width), 1) < frames

    def chunk(i, carry):
        at = pl.multiple_of(i * rows, rows)
        block = jnp.where(mask, resid_ref[pl.ds(at, rows), :].astype(f32), 0.0)
        for b in range(group):
            shifted = moved(block, b - (group - 1)).astype(bf16)
            left_ref[pl.ds(pl.multiple_of(b * neurons + at, rows), rows), :] = shifted
        return carry

    lax.fori_loop(0, neurons // rows, chunk, 0)
    block = jnp.where(mask[:features], resid_ref[neurons:, :].astype(f32), 0.0)
    left_ref[group * neurons :, :] = jnp.concatenate(
        [moved(block, b - (group - 1)) for b in range(group)], axis=0
    ).astype(bf16)
    mine = lax.axis_index("tm")
    span = steps * motifs // 4
    for p in (3, 1, 2, 0):
        first = pl.multiple_of((mine ^ p) * span, span)
        part = pl.ds(first, span)
        right = jnp.concatenate(
            [edge_ref[part, :lane], stack_ref[part, lane:], edge_ref[part, lane:]], axis=1
        )
        result = lax.dot_general(left_ref[...], right, (((1,), (1,)), ((), ())), preferred_element_type=f32)
        for a in range(span // motifs):
            for b in range(group):
                target = out_refs[p]
                l = group * a + b
                cols = slice(a * motifs, (a + 1) * motifs)
                few = group * neurons + b * features
                target[l, :neurons, :] = result[b * neurons : (b + 1) * neurons, cols].astype(target.dtype)
                target[l, neurons:, :] = result[few : few + features, cols].astype(target.dtype)


def update_motifs(factor, w_ref, v_ref, keep_ref, got_ref, far_ref, w_out_ref, v_out_ref):
    neurons = w_ref.shape[1]
    lags = w_ref.shape[0]

    def one(l, carry):
        common = far_ref[lags].astype(f32) + far_ref[lags + 1].astype(f32)
        total = keep_ref[l] + got_ref[0, l] + (far_ref[l].astype(f32) + common)
        w_out_ref[l] = jnp.maximum(w_ref[l].astype(f32) + factor * total[:neurons], 0.0).astype(bf16)
        v_out_ref[l] = jnp.maximum(v_ref[l].astype(f32) + factor * total[neurons:], 0.0).astype(bf16)
        return carry

    lax.fori_loop(0, lags, one, 0)


def relay_motifs(relay_ref, got_ref, far_ref):
    lags, rows, _ = relay_ref.shape
    for at, size in tiles(rows, 16):
        part = slice(at, at + size)
        total = relay_ref[:, part, :] + got_ref[1, :, part, :]
        mean = jnp.sum(total, axis=0) * (1.0 / lags)
        high = mean.astype(bf16)
        low = (mean - high.astype(f32)).astype(bf16)
        common = high.astype(f32) + low.astype(f32)
        for l in range(lags):
            far_ref[l, part, :] = (total[l] - common).astype(bf16)
        far_ref[lags, part, :] = high
        far_ref[lags + 1, part, :] = low


def sum_around(*refs):
    parts, out_ref = refs[:wide], refs[wide]
    total = parts[0][...]
    for part in parts[1:]:
        total = total + part[...].astype(f32)
    out_ref[...] = total.astype(out_ref.dtype)


def update(factor, active_ref, parts_ref, out_ref):
    i, y = place()
    own = active_ref[pl.ds(pl.multiple_of(y * patch, patch), patch), pl.ds(pl.multiple_of(i * lane, lane), lane)]
    total = jnp.sum(parts_ref[...].astype(f32), axis=0)
    block = jnp.maximum(own.astype(f32) + factor * total, 0.0).astype(bf16)
    for j in range(deep):
        out_ref[j] = block


def join_columns(parts_ref, out_ref):
    for j in range(deep):
        out_ref[:, lane * j : lane * (j + 1)] = parts_ref[j]


def join_rows(*refs):
    parts, out_ref = refs[:wide], refs[wide]
    _, y = place()
    for r in range(wide):
        row = pl.multiple_of((y + wide - r) % wide * patch, patch)
        out_ref[pl.ds(row, patch), :] = parts[r][...]


def call(body, out_shape, scratch, args, flops=0, moves=1 << 20, vmem=8, in_specs=None):
    if in_specs:
        args = [pltpu.with_memory_space_constraint(a, pltpu.HBM) if p is HBM else a for a, p in zip(args, in_specs)]
    return pl.pallas_call(
        body,
        out_shape=out_shape,
        in_specs=in_specs or [VMEM] * len(args),
        out_specs=jax.tree.map(lambda _: VMEM, out_shape),
        scratch_shapes=scratch,
        compiler_params=pltpu.CompilerParams(vmem_limit_bytes=vmem << 20),
        cost_estimate=pl.CostEstimate(flops=flops, bytes_accessed=moves, transcendentals=0),
    )(*args)


def local(data, behaviour, motifs, behav_motifs, activations):
    lags_here, neurons, width = motifs.shape
    features = behaviour.shape[0]
    frames = activations.shape[1]
    lags = lags_here * lax.axis_size("tm")
    all_frames = frames * lax.axis_size("tm")
    all_neurons = neurons * lax.axis_size("neuron")
    all_features = features * lax.axis_size("neuron")
    scale = 1.0 / (lags * width)
    rate_motif = 0.5 * lags * width / math.sqrt(all_frames)
    rate_active = 0.5 * lags * width / math.sqrt(lags * (all_neurons + 4 * all_features))
    shape = jax.ShapeDtypeStruct
    steps = lags // group

    w2 = crossed(motifs, 2)
    w1 = crossed(motifs, 1)
    p0, active = call(
        pack,
        [shape((pack_rows, width), bf16), shape(activations.shape, bf16)],
        [
            pltpu.VMEM(behav_motifs.shape, bf16),
            pltpu.VMEM((neurons, lane), bf16),
            pltpu.VMEM((features, lane), bf16),
            pltpu.SemaphoreType.DMA((4,)),
        ],
        [behav_motifs, activations, data, behaviour],
        in_specs=[HBM] * 4,
    )
    p3 = crossed(p0, 3)
    p2 = crossed(p0, 2)
    p1 = crossed(p0, 1)
    w3 = crossed(w2, 1)
    stack, half, turned = call(
        forward_half,
        [
            shape((steps * width, frames), bf16),
            shape((group * (neurons + features), frames + lane), f32),
            shape((group * width, steps // 2 * neurons), bf16),
        ],
        [],
        [active, motifs, w1, p0, p1],
        flops=lags * (neurons + features) * width * frames,
        moves=8 << 20,
        vmem=16,
    )

    grads_and_more = call(
        functools.partial(forward_backward, scale, frames),
        [shape((deep, patch, lane), f32 if r == 0 else bf16) for r in range(wide)]
        + [shape((neurons + features, frames + lane), bf16), shape((steps * width, 2 * lane), bf16)],
        [
            pltpu.VMEM((group * width, frames + lane), f32),
            pltpu.VMEM((lags * features, width), bf16),
            pltpu.VMEM((group * (neurons + features), frames + lane), f32),
            pltpu.VMEM((steps * neurons, frames + lane), bf16),
            pltpu.VMEM((lags * features, frames), bf16),
            pltpu.VMEM((group * width, steps * neurons), bf16),
            pltpu.VMEM((deep * wide, patch, lane), f32),
        ],
        [half, turned, stack, active, data, behaviour, motifs, w1, w2, w3, p0, p1, p2, p3],
        flops=3 * lags * (neurons + features) * width * frames,
        moves=4 << 20,
        vmem=24,
    )
    grads, resid, edges = grads_and_more[:wide], grads_and_more[wide], grads_and_more[wide + 1]
    around_parts = [grads[0]]
    for r in range(1, wide):
        around_parts.append(around(grads[r], r))

    per_lag = (lags_here, neurons + features, width)
    keep, relay, send = call(
        functools.partial(motif_gradients, frames, width),
        [shape(per_lag, f32), shape(per_lag, f32), shape((2,) + per_lag, f32)],
        [pltpu.VMEM((group * (neurons + features), frames + lane), bf16)],
        [stack, edges, resid],
        flops=2 * lags * (neurons + features) * width * frames,
        moves=4 << 20,
        vmem=8,
    )
    got = crossed(send, 1)

    sums = call(sum_around, shape((deep, patch, lane), bf16), [], around_parts)
    blocks = call(
        functools.partial(update, rate_active * scale),
        shape((deep, patch, lane), bf16),
        [],
        [active, exchanged(sums)],
    )
    far = call(
        relay_motifs,
        shape((lags_here + 2,) + per_lag[1:], bf16),
        [],
        [relay, got],
        moves=4 << 20,
    )
    far = crossed(far, 2)
    blocks = exchanged(blocks)
    strip = call(join_columns, shape((patch, frames), bf16), [], [blocks])
    rows = [strip]
    for r in range(1, wide):
        rows.append(around(strip, r))
    new_motifs, new_behav = call(
        functools.partial(update_motifs, rate_motif * scale),
        [shape(motifs.shape, bf16), shape(behav_motifs.shape, bf16)],
        [],
        [motifs, behav_motifs, keep, got, far],
        moves=4 << 20,
    )
    new_active = call(join_rows, shape((width, frames), bf16), [], rows)
    return (new_motifs, new_behav, new_active)


def solution(mesh):
    placed = (
        P("neuron", "tm"),
        P("neuron", "tm"),
        P("tm", "neuron", None),
        P("tm", "neuron", None),
        P(None, "tm"),
    )
    return jax.shard_map(
        local,
        mesh=mesh,
        in_specs=placed,
        out_specs=(P("tm", "neuron", None), P("tm", "neuron", None), P(None, "tm")),
        check_vma=False,
    )
```

```python
import functools
import math

import jax
import jax.numpy as jnp
from jax import lax
from jax.experimental import pallas as pl
from jax.experimental.pallas import tpu as pltpu
from jax.sharding import PartitionSpec as P


behaviour_weight = 2.0
lane = 128
group = 4
deep, wide = 16, 4
coarse_step = 1024
patch = 32
f32 = jnp.float32
bf16 = jnp.bfloat16
VMEM = pl.BlockSpec(memory_space=pltpu.VMEM)
HBM = pl.BlockSpec(memory_space=pltpu.HBM)


def crossed(shard, mask):
    return lax.ppermute(shard, "tm", [(i, i ^ mask) for i in range(4)])


def around(shard, by):
    pairs = [(i * wide + y, i * wide + (y + by) % wide) for i in range(deep) for y in range(wide)]
    return lax.ppermute(shard, "neuron", pairs)


def exchanged(blocks):
    groups = [[i * wide + y for i in range(deep)] for y in range(wide)]
    return lax.all_to_all(blocks, "neuron", 0, 0, axis_index_groups=groups, tiled=True)


def place():
    me = lax.axis_index("neuron")
    return me // wide, me % wide


def moved(x, by):
    by = by % x.shape[1]
    return x if by == 0 else pltpu.roll(x, x.shape[1] - by, 1)


def tiles(width, step):
    at = 0
    while at < width:
        size = min(step, width - at)
        yield at, size
        at += size


edge = 32
first_a, last_a, first_d, first_b = 64, 96, 128, 160
pack_rows = 168


def fetched(pairs, sems):
    copies = [pltpu.make_async_copy(source, target, sems.at[i]) for i, (source, target) in enumerate(pairs)]
    for copy in copies:
        copy.start()
    for copy in copies:
        copy.wait()


def pack(v_hbm, active_hbm, data_hbm, behav_hbm, w_hbm, out_ref, active_ref, w_ref, v_ref, data_ref, behav_ref, sems):
    frames = active_hbm.shape[1]
    fetched(
        [
            (active_hbm, active_ref),
            (v_hbm, v_ref),
            (data_hbm.at[:, :lane], data_ref),
            (behav_hbm.at[:, :lane], behav_ref),
            (w_hbm, w_ref),
        ],
        sems,
    )
    out_ref[:first_a] = v_ref[...].reshape(first_a, lane)
    out_ref[first_a:last_a] = active_ref[:, :lane].T[:edge]
    out_ref[last_a:first_d] = active_ref[:, frames - lane :].T[lane - edge :]
    out_ref[first_d:first_b] = data_ref[...].T[:edge]
    out_ref[first_b:] = behav_ref[...]


def nearest(odd, near_ref, far_ref, rows):
    mine = lax.axis_index("tm")
    return jnp.where(mine % 2 == odd, near_ref[rows, :], far_ref[rows, :])


def shifted_edges(near_ref, far_ref, active_ref, edge_ref):
    motifs, frames = active_ref.shape
    blank = jnp.zeros((lane - edge, lane), bf16)
    before = nearest(1, near_ref, far_ref, slice(last_a, first_d))
    before = jnp.where(lax.axis_index("tm") > 0, before, jnp.zeros_like(before))
    after = nearest(0, near_ref, far_ref, slice(first_a, last_a))
    first = jnp.concatenate([jnp.concatenate([blank, before], axis=0).T, active_ref[:, :lane]], axis=1)
    last = jnp.concatenate([active_ref[:, frames - lane :], jnp.concatenate([after, blank], axis=0).T], axis=1)
    for a in range(edge_ref.shape[0] // motifs):
        by = lane - (group - 1) - group * a
        edge_ref[a * motifs : (a + 1) * motifs, :lane] = moved(first, by)[:, :lane]
        edge_ref[a * motifs : (a + 1) * motifs, lane:] = moved(last, by)[:, :lane]


def by_lag(w_ref, pack_ref):
    lags = w_ref.shape[0]
    steps = lags // group
    rows = [jnp.concatenate([w_ref[group * a + b] for a in range(steps)], axis=1) for b in range(group)]
    few = first_a // steps
    rows.append(jnp.concatenate([pack_ref[few * a : few * (a + 1), :] for a in range(steps)], axis=1))
    return jnp.concatenate(rows, axis=0)


def forward_half(active_ref, w0_ref, w1_ref, p0_ref, p1_ref, stack_ref, out_ref, turned_ref):
    motifs, frames = active_ref.shape
    rows = 16

    def chunk(i, carry):
        at = pl.multiple_of(i * rows, rows)
        block = active_ref[pl.ds(at, rows), :]
        for a in range(stack_ref.shape[0] // motifs):
            shifted = moved(block, -(group - 1) - group * a)
            stack_ref[pl.ds(pl.multiple_of(a * motifs + at, rows), rows), :] = shifted
        return carry

    lax.fori_loop(0, motifs // rows, chunk, 0)

    mine = lax.axis_index("tm")
    span = stack_ref.shape[0] // 4
    left = jnp.concatenate([by_lag(w0_ref, p0_ref), by_lag(w1_ref, p1_ref)], axis=1)
    starts = [pl.multiple_of((mine ^ p) * span, span) for p in (0, 1)]
    for at, size in list(tiles(frames, 256))[1:]:
        cols = slice(at, at + size)
        right = jnp.concatenate([stack_ref[pl.ds(start, span), cols] for start in starts], axis=0)
        out_ref[:, cols] = jnp.dot(left, right, preferred_element_type=f32)
        if at == 256:
            _, neurons, motifs = w0_ref.shape
            for p, w_ref in enumerate((w0_ref, w1_ref)):
                for a in range(span // motifs):
                    first = p * span + a * neurons
                    for b in range(group):
                        turned_ref[b * motifs : (b + 1) * motifs, first : first + neurons] = w_ref[group * a + b].T


def forward_backward(scale, frames, *refs):
    base_ref, turned_ref, stack_ref, active_ref, data_ref, behav_ref = refs[:6]
    w_parts, packs = refs[6:10], refs[10:14]
    grad_refs, resid_ref, edge_ref = refs[14:18], refs[18], refs[19]
    late_ref, v_ref, out_ref, back_ref, few_ref, turn_ref, sum_ref = refs[20:]
    part, neurons, motifs = w_parts[0].shape
    lags = 4 * part
    features = v_ref.shape[0] // lags
    steps = lags // group
    width = frames + lane
    mine = lax.axis_index("tm")
    _, y = place()
    valid = mine < 3
    parts = list(tiles(width, 256))

    def reach(at, size):
        return slice(at, min(at + size + lane, width))

    shifted_edges(packs[1], packs[3], active_ref, edge_ref)
    lefts = [by_lag(w, p) for w, p in zip(w_parts, packs)]
    span = stack_ref.shape[0] // 4
    starts = [pl.multiple_of((mine ^ p) * span, span) for p in range(4)]
    after = nearest(0, packs[1], packs[3], slice(first_d, first_b))
    after = jnp.concatenate([after, jnp.zeros((lane - edge, lane), bf16)], axis=0).T
    after_few = nearest(0, packs[1], packs[3], slice(first_b, pack_rows))

    def shifted(p, at, size):
        rows = pl.ds(starts[p], span)
        if at == 0:
            return jnp.concatenate([edge_ref[rows, :lane], stack_ref[rows, lane:size]], axis=1)
        return edge_ref[rows, lane:] if at >= frames else stack_ref[rows, at : at + size]

    def product(at, size):
        cols = slice(at, at + size)
        whole = at == 0 or at >= frames
        these = range(4) if whole else (2, 3)
        left = jnp.concatenate([lefts[p] for p in these], axis=1)
        right = jnp.concatenate([shifted(p, at, size) for p in these], axis=0)
        part = jnp.dot(left, right, preferred_element_type=f32)
        out_ref[:, cols] = part if whole else part + base_ref[:, cols]

    def recon(first, count, at, size):
        total = None
        for b in range(group):
            rows = slice(first + b * count, first + (b + 1) * count)
            term = moved(out_ref[rows, reach(at, size)], group - 1 - b)[:, :size]
            total = term if total is None else total + term
        return scale * total

    def residual(at, size):
        cols = slice(at, at + size)
        past = at >= frames
        own = after if past else data_ref[:, cols]
        own_few = after_few if past else behav_ref[:, cols]
        resid = own.astype(f32) - recon(0, neurons, at, size)
        few = behaviour_weight * (own_few.astype(f32) - recon(group * neurons, features, at, size))
        if past:
            resid, few = jnp.where(valid, resid, 0.0), jnp.where(valid, few, 0.0)
        resid_ref[:neurons, cols] = resid.astype(bf16)
        resid_ref[neurons:, cols] = few.astype(bf16)

    def spread(at, size):
        block = resid_ref[:neurons, reach(at, size)]
        for a in range(steps):
            back_ref[a * neurons : (a + 1) * neurons, at : at + size] = moved(block, group * a)[:, :size]

    done = []
    coarse = list(tiles(width, coarse_step))
    for i, (at, size) in enumerate(parts):
        product(at, size)
        if i == 0:
            for p in range(4):
                v_ref[pl.ds(pl.multiple_of((mine ^ p) * first_a, first_a), first_a)] = packs[p][:first_a, :]
                for a in range(part // group):
                    column = pl.multiple_of((mine ^ p) * span + a * neurons, neurons)
                    for b in range(group):
                        if p < 2:
                            turned = turned_ref[
                                b * motifs : (b + 1) * motifs, p * span + a * neurons : p * span + (a + 1) * neurons
                            ]
                        else:
                            turned = w_parts[p][group * a + b].T
                        turn_ref[b * motifs : (b + 1) * motifs, pl.ds(column, neurons)] = turned
        while len(done) < len(coarse) and (
            reach(*coarse[len(done)]).stop <= at + size
        ):
            residual(*coarse[len(done)])
            if done:
                spread(*coarse[len(done) - 1])
            done.append(at)
    spread(*coarse[-1])

    few = resid_ref[neurons:, :].astype(f32)
    for l in range(0, lags, 2):
        pair = jnp.concatenate([moved(few, l)[:, :frames], moved(few, l + 1)[:, :frames]], axis=0)
        few_ref[l * features : (l + 2) * features, :] = pair.astype(bf16)
    v_left = v_ref[...].T

    def gradient(at, size):
        total = jnp.dot(v_left, few_ref[:, at : at + size], preferred_element_type=f32)
        for b in range(group):
            term = late_ref[b * motifs : (b + 1) * motifs, reach(at, size)]
            total = total + moved(term, b)[:, :size]
        for i in range(motifs // patch):
            for j in range(size // lane):
                sum_ref[i * (frames // lane) + at // lane + j] = total[
                    patch * i : patch * (i + 1), lane * j : lane * (j + 1)
                ]

    waiting = list(tiles(frames, coarse_step))
    for at, size in parts:
        cols = slice(at, at + size)
        late_ref[:, cols] = jnp.dot(turn_ref[...], back_ref[:, cols], preferred_element_type=f32)
        while waiting and reach(*waiting[0]).stop <= at + size:
            gradient(*waiting.pop(0))
    for r in range(wide):
        peer = (y + r) % wide
        grad_refs[r][...] = sum_ref[pl.ds(peer * deep, deep)].astype(grad_refs[r].dtype)


def motif_gradients(frames, motifs, stack_ref, edge_ref, resid_ref, keep_ref, relay_ref, send_ref, left_ref):
    out_refs = (keep_ref, send_ref.at[0], relay_ref, send_ref.at[1])
    features = keep_ref.shape[1] - 128
    neurons = resid_ref.shape[0] - features
    steps = stack_ref.shape[0] // motifs
    width = frames + lane
    rows = 16
    mask = lax.broadcasted_iota(jnp.int32, (rows, width), 1) < frames

    def chunk(i, carry):
        at = pl.multiple_of(i * rows, rows)
        block = jnp.where(mask, resid_ref[pl.ds(at, rows), :].astype(f32), 0.0)
        for b in range(group):
            shifted = moved(block, b - (group - 1)).astype(bf16)
            left_ref[pl.ds(pl.multiple_of(b * neurons + at, rows), rows), :] = shifted
        return carry

    lax.fori_loop(0, neurons // rows, chunk, 0)
    block = jnp.where(mask[:features], resid_ref[neurons:, :].astype(f32), 0.0)
    left_ref[group * neurons :, :] = jnp.concatenate(
        [moved(block, b - (group - 1)) for b in range(group)], axis=0
    ).astype(bf16)
    mine = lax.axis_index("tm")
    span = steps * motifs // 4
    for p in (3, 1, 2, 0):
        first = pl.multiple_of((mine ^ p) * span, span)
        part = pl.ds(first, span)
        right = jnp.concatenate(
            [edge_ref[part, :lane], stack_ref[part, lane:], edge_ref[part, lane:]], axis=1
        )
        result = lax.dot_general(left_ref[...], right, (((1,), (1,)), ((), ())), preferred_element_type=f32)
        for a in range(span // motifs):
            for b in range(group):
                target = out_refs[p]
                l = group * a + b
                cols = slice(a * motifs, (a + 1) * motifs)
                few = group * neurons + b * features
                target[l, :neurons, :] = result[b * neurons : (b + 1) * neurons, cols].astype(target.dtype)
                target[l, neurons:, :] = result[few : few + features, cols].astype(target.dtype)


def update_motifs(factor, w_ref, v_ref, keep_ref, got_ref, far_ref, w_out_ref, v_out_ref):
    neurons = w_ref.shape[1]
    lags = w_ref.shape[0]

    def one(l, carry):
        common = far_ref[lags].astype(f32) + far_ref[lags + 1].astype(f32)
        total = keep_ref[l] + got_ref[0, l] + (far_ref[l].astype(f32) + common)
        w_out_ref[l] = jnp.maximum(w_ref[l].astype(f32) + factor * total[:neurons], 0.0).astype(bf16)
        v_out_ref[l] = jnp.maximum(v_ref[l].astype(f32) + factor * total[neurons:], 0.0).astype(bf16)
        return carry

    lax.fori_loop(0, lags, one, 0)


def relay_motifs(relay_ref, got_ref, far_ref):
    lags, rows, _ = relay_ref.shape
    for at, size in tiles(rows, 16):
        part = slice(at, at + size)
        total = relay_ref[:, part, :] + got_ref[1, :, part, :]
        mean = jnp.sum(total, axis=0) * (1.0 / lags)
        high = mean.astype(bf16)
        low = (mean - high.astype(f32)).astype(bf16)
        common = high.astype(f32) + low.astype(f32)
        for l in range(lags):
            far_ref[l, part, :] = (total[l] - common).astype(bf16)
        far_ref[lags, part, :] = high
        far_ref[lags + 1, part, :] = low


def sum_around(*refs):
    parts, out_ref = refs[:wide], refs[wide]
    total = parts[0][...]
    for part in parts[1:]:
        total = total + part[...].astype(f32)
    out_ref[...] = total.astype(out_ref.dtype)


def update(factor, active_ref, parts_ref, out_ref):
    i, y = place()
    own = active_ref[pl.ds(pl.multiple_of(y * patch, patch), patch), pl.ds(pl.multiple_of(i * lane, lane), lane)]
    total = jnp.sum(parts_ref[...].astype(f32), axis=0)
    block = jnp.maximum(own.astype(f32) + factor * total, 0.0).astype(bf16)
    for j in range(deep):
        out_ref[j] = block


def join_columns(parts_ref, out_ref):
    for j in range(deep):
        out_ref[:, lane * j : lane * (j + 1)] = parts_ref[j]


def join_rows(*refs):
    parts, out_hbm, sems = refs[:wide], refs[wide], refs[wide + 1]
    _, y = place()
    targets = [out_hbm.at[pl.ds(pl.multiple_of((y + wide - r) % wide * patch, patch), patch)] for r in range(wide)]
    fetched(list(zip(parts, targets)), sems)


def call(body, out_shape, scratch, args, flops=0, moves=1 << 20, vmem=8, in_specs=None, out_specs=None):
    if in_specs:
        args = [pltpu.with_memory_space_constraint(a, pltpu.HBM) if p is HBM else a for a, p in zip(args, in_specs)]
    return pl.pallas_call(
        body,
        out_shape=out_shape,
        in_specs=in_specs or [VMEM] * len(args),
        out_specs=out_specs or jax.tree.map(lambda _: VMEM, out_shape),
        scratch_shapes=scratch,
        compiler_params=pltpu.CompilerParams(vmem_limit_bytes=vmem << 20),
        cost_estimate=pl.CostEstimate(flops=flops, bytes_accessed=moves, transcendentals=0),
    )(*args)


def local(data, behaviour, motifs, behav_motifs, activations):
    lags_here, neurons, width = motifs.shape
    features = behaviour.shape[0]
    frames = activations.shape[1]
    lags = lags_here * lax.axis_size("tm")
    all_frames = frames * lax.axis_size("tm")
    all_neurons = neurons * lax.axis_size("neuron")
    all_features = features * lax.axis_size("neuron")
    scale = 1.0 / (lags * width)
    rate_motif = 0.5 * lags * width / math.sqrt(all_frames)
    rate_active = 0.5 * lags * width / math.sqrt(lags * (all_neurons + 4 * all_features))
    shape = jax.ShapeDtypeStruct
    steps = lags // group

    w2 = crossed(motifs, 2)
    w1 = crossed(motifs, 1)
    p0, active, w0 = call(
        pack,
        [shape((pack_rows, width), bf16), shape(activations.shape, bf16), shape(motifs.shape, bf16)],
        [
            pltpu.VMEM(behav_motifs.shape, bf16),
            pltpu.VMEM((neurons, lane), bf16),
            pltpu.VMEM((features, lane), bf16),
            pltpu.SemaphoreType.DMA((5,)),
        ],
        [behav_motifs, activations, data, behaviour, motifs],
        in_specs=[HBM] * 5,
    )
    p3 = crossed(p0, 3)
    p2 = crossed(p0, 2)
    p1 = crossed(p0, 1)
    w3 = crossed(w2, 1)
    stack, half, turned = call(
        forward_half,
        [
            shape((steps * width, frames), bf16),
            shape((group * (neurons + features), frames + lane), f32),
            shape((group * width, steps // 2 * neurons), bf16),
        ],
        [],
        [active, w0, w1, p0, p1],
        flops=lags * (neurons + features) * width * frames,
        moves=8 << 20,
        vmem=16,
    )

    grads_and_more = call(
        functools.partial(forward_backward, scale, frames),
        [shape((deep, patch, lane), f32 if r == 0 else bf16) for r in range(wide)]
        + [shape((neurons + features, frames + lane), bf16), shape((steps * width, 2 * lane), bf16)],
        [
            pltpu.VMEM((group * width, frames + lane), f32),
            pltpu.VMEM((lags * features, width), bf16),
            pltpu.VMEM((group * (neurons + features), frames + lane), f32),
            pltpu.VMEM((steps * neurons, frames + lane), bf16),
            pltpu.VMEM((lags * features, frames), bf16),
            pltpu.VMEM((group * width, steps * neurons), bf16),
            pltpu.VMEM((deep * wide, patch, lane), f32),
        ],
        [half, turned, stack, active, data, behaviour, w0, w1, w2, w3, p0, p1, p2, p3],
        flops=3 * lags * (neurons + features) * width * frames,
        moves=4 << 20,
        vmem=24,
    )
    grads, resid, edges = grads_and_more[:wide], grads_and_more[wide], grads_and_more[wide + 1]
    around_parts = [grads[0]]
    for r in range(1, wide):
        around_parts.append(around(grads[r], r))

    per_lag = (lags_here, neurons + features, width)
    keep, relay, send = call(
        functools.partial(motif_gradients, frames, width),
        [shape(per_lag, f32), shape(per_lag, f32), shape((2,) + per_lag, f32)],
        [pltpu.VMEM((group * (neurons + features), frames + lane), bf16)],
        [stack, edges, resid],
        flops=2 * lags * (neurons + features) * width * frames,
        moves=4 << 20,
        vmem=8,
    )
    got = crossed(send, 1)

    sums = call(sum_around, shape((deep, patch, lane), bf16), [], around_parts)
    blocks = call(
        functools.partial(update, rate_active * scale),
        shape((deep, patch, lane), bf16),
        [],
        [active, exchanged(sums)],
    )
    far = call(
        relay_motifs,
        shape((lags_here + 2,) + per_lag[1:], bf16),
        [],
        [relay, got],
        moves=4 << 20,
    )
    far = crossed(far, 2)
    blocks = exchanged(blocks)
    strip = call(join_columns, shape((patch, frames), bf16), [], [blocks])
    rows = [strip]
    for r in range(1, wide):
        rows.append(around(strip, r))
    new_motifs, new_behav = call(
        functools.partial(update_motifs, rate_motif * scale),
        [shape(motifs.shape, bf16), shape(behav_motifs.shape, bf16)],
        [],
        [w0, behav_motifs, keep, got, far],
        moves=4 << 20,
    )
    new_active = call(
        join_rows, shape((width, frames), bf16), [pltpu.SemaphoreType.DMA((wide,))], rows, out_specs=HBM
    )
    return (new_motifs, new_behav, new_active)


def solution(mesh):
    placed = (
        P("neuron", "tm"),
        P("neuron", "tm"),
        P("tm", "neuron", None),
        P("tm", "neuron", None),
        P(None, "tm"),
    )
    return jax.shard_map(
        local,
        mesh=mesh,
        in_specs=placed,
        out_specs=(P("tm", "neuron", None), P("tm", "neuron", None), P(None, "tm")),
        check_vma=False,
    )
```
